128 devices in a mesh: dev: 128 (over y, x, z, core).
Axes of the slice: x: 4, y: 4, z: 4, core: 2. Of those that a mesh axis runs over, the one named last changes fastest.
Arguments:
- embeddings: bfloat16 [32768, 1024], P('dev'), may hold values from -6 to 6
- cluster_id: int32 [32768], P('dev'), may hold values from 0 to 15, as said below
- requests: int32 [16384], P('dev'), may hold values from -1 to 1, as said below
- pair_left: int32 [49152], P('dev'), may hold values from 0 to 127, as said below
- pair_right: int32 [49152], P('dev'), may hold values from 0 to 127, as said below
Outputs:
- best: float32 [32768], P('dev')
The draws below stay inside these ranges and needn't reach their ends.
Inputs may be any that keep to these rules, and one draw needn't show every extreme that they name: Rows are sorted by cluster: cluster_id never falls along the rows, and every cluster has rows. Every slot that some task of device d names has a block (requests at least 0 there); a device's tasks name slots of at most 40 consecutive owners. pair_left <= pair_right for every task; no device lists one slot pair twice. `pair_right`: see pair_left.
All inputs are finite; a program needn't handle non-finite values.
Results may differ from the reference program's by a relative error of at most 0.00086.
Values may be sent and summed in bfloat16 or wider, within the bound.
A program may use at most 192 MiB of HBM per device.

```python
import jax
import jax.numpy as jnp
from jax import lax

D = 1024
BLOCK = 128
BLK_DEV = 2
PAIRS = 384
GROUP = 64
CLUSTERS = 16
NBLK = 256
ROWS = 32768
N_DEV = 128


def cluster_bounds(key):
    base = jax.random.fold_in(key, 31)
    order = jax.random.permutation(jax.random.fold_in(base, 1), CLUSTERS).astype(jnp.int32)
    weights = jnp.int32(5040) // (order + 1)
    running = jnp.cumsum(weights).astype(jnp.int32)
    total = running[-1]
    bounds = running[:-1] * ROWS // total
    jitter = jax.random.randint(jax.random.fold_in(base, 2), (CLUSTERS - 1,), -(BLOCK // 4), BLOCK // 4 + 1).astype(jnp.int32)
    return (bounds + jitter).astype(jnp.int32)


def draw_cluster_id(key, part):
    bounds = cluster_bounds(key)
    rows_all = jnp.arange(ROWS, dtype=jnp.int32)
    return jnp.sum((rows_all[:, None] >= bounds[None, :]).astype(jnp.int32), axis=1).astype(jnp.int32)


def device_plan(key, device):
    width = min(N_DEV, 40)
    tri_left, tri_right = jnp.triu_indices(width)
    tri_left = tri_left.astype(jnp.int32)
    tri_right = tri_right.astype(jnp.int32)
    total = tri_left.shape[0]
    inner = jax.random.permutation(jax.random.fold_in(key, 1), total - 2)[:PAIRS - 2].astype(jnp.int32) + 1
    codes = jnp.concatenate([jnp.array([0, total - 1], dtype=jnp.int32), inner])
    codes = jax.random.permutation(jax.random.fold_in(key, 2), codes)
    drawn_start = jax.random.randint(jax.random.fold_in(key, 4), (), 0, N_DEV - width + 1).astype(jnp.int32)
    first_start = jnp.where(device == 0, jnp.int32(0), drawn_start)
    window_start = jnp.where(device == N_DEV - 1, jnp.int32(N_DEV - width), first_start)
    left = window_start + tri_left[codes]
    right = window_start + tri_right[codes]
    live = jnp.zeros((N_DEV,), jnp.int32).at[left].set(1).at[right].set(1)
    chosen = jax.random.randint(jax.random.fold_in(key, 3), (N_DEV,), 0, BLK_DEV).astype(jnp.int32)
    asks = jnp.where(live > 0, chosen, jnp.int32(-1))
    return (asks, left, right)


def whole_plan(key):
    base = jax.random.fold_in(key, 77)
    devices_all = jnp.arange(N_DEV, dtype=jnp.int32)
    keys = jax.vmap(lambda device: jax.random.fold_in(base, device))(devices_all)
    return jax.vmap(device_plan)(keys, devices_all)


def draw_requests(key, part):
    return whole_plan(key)[0].reshape(-1)


def draw_pair_left(key, part):
    return whole_plan(key)[1].reshape(-1)


def draw_pair_right(key, part):
    return whole_plan(key)[2].reshape(-1)


def levels(key, shape, split, low, top_value):
    factor_of, own = 1.0, jax.random.fold_in(key, 6)
    for axis_at, shards_of in split:
        heights = jnp.exp(jax.random.uniform(jax.random.fold_in(own, axis_at), (shards_of,), jnp.float32, low / len(split), top_value / len(split)))
        factor_of = factor_of * jnp.repeat(heights, shape[axis_at] // shards_of).reshape([-1 if axis == axis_at else 1 for axis in range(len(shape))])
    return factor_of


def bell_draw(own_key, dims, deviation, reach, pieces=(), kind=jnp.bfloat16):
    drawn = jax.random.normal(own_key, dims, jnp.float32) * deviation
    if len(pieces) > 0:
        drawn = levels(own_key, dims, pieces, -0.22, 0.18) * drawn
    return jnp.clip(drawn, min=-reach, max=reach).astype(kind)


def setup_inputs(seed: int = 0) -> dict:
    seeds = jax.random.split(jax.random.key(seed), 6)
    return {
        "embeddings": bell_draw(seeds[0], (ROWS, D), 1.0, 6.0, ((0, 128),)),
        "cluster_id": draw_cluster_id(jax.random.fold_in(seeds[5], 71), 0),
        "requests": draw_requests(jax.random.fold_in(seeds[5], 71), 0),
        "pair_left": draw_pair_left(jax.random.fold_in(seeds[5], 71), 0),
        "pair_right": draw_pair_right(jax.random.fold_in(seeds[5], 71), 0),
    }


def reference(embeddings, cluster_id, requests, pair_left, pair_right):
    values = embeddings.astype(jnp.float32)
    unit = (values * lax.rsqrt(lax.optimization_barrier(jnp.sum(values * values, axis=-1, keepdims=True)) + 1e-06)).astype(jnp.bfloat16)
    unit_blocks = unit.reshape(NBLK, BLOCK, D)
    labels = cluster_id.reshape(NBLK, BLOCK)
    table = requests.reshape(N_DEV, N_DEV)
    owners = jnp.repeat(jnp.arange(N_DEV, dtype=jnp.int32), PAIRS)
    block_left = (pair_left * BLK_DEV + table[owners, pair_left]).astype(jnp.int32)
    block_right = (pair_right * BLK_DEV + table[owners, pair_right]).astype(jnp.int32)
    diagonal_mask = jnp.eye(BLOCK, dtype=bool)

    def step(carry, indices):
        left, right = indices
        first = unit_blocks[left].astype(jnp.float32)
        second = unit_blocks[right].astype(jnp.float32)
        sims = jnp.einsum('gid,gjd->gij', first, second)
        same = labels[left][:, :, None] == labels[right][:, None, :]
        selfish = (left == right)[:, None, None] & diagonal_mask[None]
        sims = jnp.where(same & ~selfish, sims, jnp.float32(-1.0))
        carry = carry.at[left].max(lax.optimization_barrier(jnp.max(sims, axis=2)))
        carry = carry.at[right].max(lax.optimization_barrier(jnp.max(sims, axis=1)))
        return (carry, None)
    start = jnp.full((NBLK, BLOCK), -1.0, jnp.float32)
    result, _ = lax.scan(step, start, (block_left.reshape(-1, GROUP), block_right.reshape(-1, GROUP)))
    return result.reshape(ROWS)
```

```python
import functools

import jax
import jax.numpy as jnp
from jax import lax
from jax.experimental import pallas as pl
from jax.experimental.pallas import tpu as pltpu
from jax.sharding import PartitionSpec as P

BLOCK = 128
LINES = 16
DELTAS = (-1, 4, -3, 5, -2)
NV = len(DELTAS)
MESH = pl.DeviceIdType.MESH
F32 = jnp.float32
BF16 = jnp.bfloat16


def iota(shape, axis):
    return lax.broadcasted_iota(jnp.int32, shape, axis)


def dot_nt(a, b):
    return lax.dot_general(a, b, (((1,), (1,)), ((), ())), preferred_element_type=F32)


def dot_nn(a, b):
    return lax.dot_general(a, b, (((1,), (0,)), ((), ())), preferred_element_type=F32)


def onehot(mask):
    return jnp.where(mask, F32(1.0), F32(0.0)).astype(BF16)


def kernel(
    emb_ref, lab_ref, req_ref, pl_ref, pr_ref, out_ref,
    line, vis, wout, win, pout, pin, lcol, elab, racc, cacc, rout, rin, cout, cin,
    z_send, z_recv, p_send, p_recv, v_send, v_recv, w_send, w_recv, q_send, q_recv,
    r_send, r_recv, c_send, c_recv,
):
    rows = emb_ref.shape[0]
    half = rows // 2
    me = lax.axis_index("dev")
    core = lax.rem(me, 2)
    z = lax.rem(me // 2, 4)
    ln = me // 8

    def dev(dl, dz, dk):
        to_l = lax.rem(ln + dl + LINES, LINES)
        to_z = lax.rem(z + dz, 4)
        to_k = lax.rem(core + dk, 2)
        return to_l * 8 + to_z * 2 + to_k

    barrier = pltpu.get_barrier_semaphore()
    peers = [dev(0, s % 4, s // 4) for s in range(1, 8)] + [dev(j, 0, 0) for j in range(1, LINES)]
    for peer in peers:
        pl.semaphore_signal(barrier, inc=1, device_id=(peer,), device_id_type=MESH)

    def remote(src, dst, send, recv, to):
        return pltpu.make_async_remote_copy(
            src_ref=src, dst_ref=dst, send_sem=send, recv_sem=recv, device_id=(to,), device_id_type=MESH
        )

    @pl.loop(0, rows // 64)
    def _(i):
        at = pl.ds(pl.multiple_of(i * 64, 64), 64)
        x = emb_ref[at, :].astype(F32)
        total = jnp.sum(x * x, axis=1, keepdims=True)
        line[0, at, :] = (x * lax.rsqrt(total + 1e-06)).astype(BF16)

    expand = onehot((iota((256, 128), 0) // 2 == iota((256, 128), 1)) & (req_ref[...] == iota((256, 128), 0) % 2))
    left = dot_nn(expand, onehot(iota((128, pl_ref.shape[1]), 0) == pl_ref[...])).astype(BF16)
    right = dot_nn(expand, onehot(iota((128, pr_ref.shape[1]), 0) == pr_ref[...])).astype(BF16)
    want = (dot_nt(left, right) + dot_nt(right, left)).astype(BF16)
    labels = jnp.broadcast_to(lab_ref[...].astype(F32), (16, rows)).astype(BF16)
    for j in range(LINES):
        wout[j, 0:16, :] = want[16 * j : 16 * j + 16, :]
        wout[j, 16:32, :] = labels

    pl.semaphore_wait(barrier, len(peers))

    up_a = remote(line.at[0, 0:half], line.at[3, 0:half], z_send.at[0], z_recv.at[0], dev(0, 1, 0))
    dn_b = remote(line.at[0, half:rows], line.at[1, half:rows], z_send.at[1], z_recv.at[1], dev(0, 3, 0))
    up_b = remote(line.at[0, half:rows], line.at[3, half:rows], z_send.at[2], z_recv.at[2], dev(0, 1, 0))
    dn_a = remote(line.at[0, 0:half], line.at[1, 0:half], z_send.at[3], z_recv.at[3], dev(0, 3, 0))
    far_a = remote(line.at[3, 0:half], line.at[2, 0:half], z_send.at[4], z_recv.at[4], dev(0, 1, 0))
    far_b = remote(line.at[1, half:rows], line.at[2, half:rows], z_send.at[5], z_recv.at[5], dev(0, 3, 0))
    share = [
        remote(line.at[r], line.at[4 + r], p_send.at[r], p_recv.at[r], dev(0, 0, 1)) for r in range(4)
    ]
    visits = [
        remote(
            line.at[0] if d != -2 else vis.at[DELTAS.index(-1)],
            vis.at[m], v_send.at[m], v_recv.at[m],
            dev(-d if d != -2 else 1, 0, 0),
        )
        for m, d in enumerate(DELTAS)
    ]
    tell = [
        remote(
            wout.at[lax.rem(ln + j, LINES)], win.at[LINES - j], w_send.at[j], w_recv.at[LINES - j], dev(j, 0, 0)
        )
        for j in range(1, LINES)
    ]
    back = [(4 - s % 4) % 4 + 4 * (s // 4) for s in range(8)]
    pool = [
        remote(pout, pin.at[back[s]], q_send.at[s], q_recv.at[back[s]], dev(0, s % 4, s // 4)) for s in range(1, 8)
    ]

    for copy in tell:
        copy.start()
    up_a.start()
    dn_b.start()
    share[0].start()
    up_b.start()
    dn_a.start()
    for m, d in enumerate(DELTAS):
        if d != -2:
            visits[m].start()

    total = wout[ln, 0:16, :].astype(F32)
    for copy in tell:
        copy.wait_recv()
    for j in range(1, LINES):
        total = total + win[j, 0:16, :].astype(F32)
    pout[0:16, :] = total.astype(BF16)
    pout[16:32, :] = labels
    for copy in pool:
        copy.start()

    up_a.wait_recv()
    far_a.start()
    dn_b.wait_recv()
    far_b.start()

    for copy in pool:
        copy.wait_recv()
    for s in range(1, 8):
        total = total + pin[s, 0:16, :].astype(F32)
    total = total.astype(BF16)

    eye = iota((BLOCK, BLOCK), 0) == iota((BLOCK, BLOCK), 1)
    ones = jnp.full((BLOCK, BLOCK), 1.0, BF16)
    for s in range(8):
        row = labels[0:1, :] if s == 0 else pin[s, 16:32, :][0:1, :]
        for h in range(2):
            diag = jnp.where(eye, jnp.broadcast_to(row[:, h * BLOCK : (h + 1) * BLOCK].astype(F32), (BLOCK, BLOCK)), F32(0.0))
            lcol[2 * s + h] = dot_nn(diag.astype(BF16), ones)

    for m in range(NV + 1):
        d = 0 if m == 0 else DELTAS[m - 1]
        owner = dev(d, 0, 0)
        pick = onehot(iota((256, rows), 0) == owner * 2 + iota((256, rows), 1) // BLOCK)
        listed = dot_nn(total, pick)
        mine = (labels if m == 0 else win[d % LINES, 16:32, :]).astype(F32)
        elab[m] = jnp.where(listed > 0.5, mine, F32(-1.0))

    visits[DELTAS.index(-1)].wait_recv()
    visits[DELTAS.index(-2)].start()
    up_b.wait_recv()
    share[3].start()
    dn_a.wait_recv()
    share[1].start()
    far_a.wait_recv()
    far_b.wait_recv()
    share[2].start()

    racc[...] = jnp.full(racc.shape, -1.0, F32)

    def tile(m, s, rhs):
        sims = dot_nt(line[s], rhs[...])
        base = (lax.rem(z + s % 4, 4) * 2 + lax.rem(core + s // 4, 2)) * 2
        cols = []
        for h in range(2):
            lc = lcol[2 * s + h]
            tags = elab[m, pl.ds(base + h, 1), :]
            best = None
            parts = []
            for q in range(2):
                at = slice(q * BLOCK, (q + 1) * BLOCK)
                same = lc == tags[:, at]
                if m == 0 and h == q:
                    same = same & jnp.logical_not(eye & (s == 0))
                val = jnp.where(same, sims[h * BLOCK : (h + 1) * BLOCK, at], F32(-1.0))
                best = val if best is None else jnp.maximum(best, val)
                parts.append(jnp.max(val.reshape(16, 8, BLOCK), axis=0))
            if m > 0:
                racc[2 * s + h] = jnp.maximum(racc[2 * s + h], best)
            cols.append(jnp.concatenate(parts, axis=1))
        cacc[m] = jnp.maximum(cacc[m], jnp.maximum(cols[0], cols[1]))

    def column(m, rhs):
        cacc[m] = jnp.full(cacc.shape[1:], -1.0, F32)

        @pl.loop(0, 8)
        def _(s):
            tile(m, s, rhs)

        top = jnp.max(cacc[m], axis=0, keepdims=True)
        cout[m, 0:1, :] = top[:, 0:BLOCK]
        cout[m, 1:2, :] = top[:, BLOCK:]

    for copy in share:
        copy.wait_recv()
    column(0, line.at[0])
    give = []
    for m, d in enumerate(DELTAS):
        if d != -1:
            visits[m].wait_recv()
        column(m + 1, vis.at[m])
        copy = remote(cout.at[m + 1], cin.at[m], c_send.at[m], c_recv.at[m], dev(d, 0, 0))
        copy.start()
        give.append(copy)

    order = [1, 2, 3, 4, 5, 6, 7, 0]
    for s in order:
        for h in range(2):
            flat = jnp.max(jnp.transpose(racc[2 * s + h]), axis=0, keepdims=True)
            rout[s, h : h + 1, :] = flat
        if s > 0:
            copy = remote(rout.at[s], rin.at[back[s]], r_send.at[s], r_recv.at[back[s]], dev(0, s % 4, s // 4))
            copy.start()
            give.append(copy)

    result = jnp.maximum(rout[0], cout[0])
    for copy in give:
        copy.wait_recv()
    for m in range(NV):
        result = jnp.maximum(result, cin[m])
    for s in range(1, 8):
        result = jnp.maximum(result, rin[s])
    out_ref[...] = result
    for copy in [up_a, up_b, dn_a, dn_b, far_a, far_b] + share + visits + tell + pool + give:
        copy.wait_send()


def local(embeddings, cluster_id, requests, pair_left, pair_right):
    rows, width = embeddings.shape
    dma = pltpu.SemaphoreType.DMA
    vmem = pltpu.VMEM
    scratch = [
        vmem((8, rows, width), BF16),
        vmem((NV, rows, width), BF16),
        vmem((LINES, 32, 256), BF16),
        vmem((LINES, 32, 256), BF16),
        vmem((32, 256), BF16),
        vmem((8, 32, 256), BF16),
        vmem((16, BLOCK, BLOCK), F32),
        vmem((NV + 1, 16, rows), F32),
        vmem((16, BLOCK, BLOCK), F32),
        vmem((NV + 1, 8, rows), F32),
        vmem((8, 2, BLOCK), F32),
        vmem((8, 2, BLOCK), F32),
        vmem((NV + 1, 2, BLOCK), F32),
        vmem((NV, 2, BLOCK), F32),
    ]
    for count in (6, 4, NV, LINES, 8, 8, NV):
        scratch += [dma((count,)), dma((count,))]
    best = pl.pallas_call(
        kernel,
        out_shape=jax.ShapeDtypeStruct((2, BLOCK), F32),
        in_specs=[pl.BlockSpec(memory_space=pltpu.VMEM)] * 5,
        out_specs=pl.BlockSpec(memory_space=pltpu.VMEM),
        scratch_shapes=scratch,
        compiler_params=pltpu.CompilerParams(
            collective_id=0, has_side_effects=True, vmem_limit_bytes=48 * 1024 * 1024
        ),
        name="band",
    )(
        embeddings,
        cluster_id.reshape(1, -1),
        requests.reshape(1, -1),
        pair_left.reshape(1, -1),
        pair_right.reshape(1, -1),
    )
    return best.reshape(-1)


def solution(mesh):
    in_specs = (P("dev", None), P("dev"), P("dev"), P("dev"), P("dev"))
    out_specs = P("dev")
    return jax.shard_map(local, mesh=mesh, in_specs=in_specs, out_specs=out_specs, check_vma=False)
```

```python
import functools

import jax
import jax.numpy as jnp
from jax import lax
from jax.experimental import pallas as pl
from jax.experimental.pallas import tpu as pltpu
from jax.sharding import PartitionSpec as P

BLOCK = 128
LINES = 16
DELTAS = (4, 1, 3, 5, 2)
NV = len(DELTAS)
CHUNKS = 2
SPREAD = (
    (0, 0, 0, -1, 4),
    (1, 0, -1, 0, 1),
    (1, 0, 0, -1, 4),
    (2, 0, -1, 0, 1),
    (2, 0, 0, -1, 4),
    (3, 0, 1, 0, 3),
    (3, 0, -1, 0, 1),
    (3, 0, 0, -1, 4),
    (0, 4, 1, 0, 3),
    (0, 4, -1, 0, 1),
    (1, 4, 1, 0, 3),
    (2, 4, 1, 0, 3),
    (3, 4, -1, 0, 5),
    (0, 1, 0, -1, 5),
    (1, 1, -1, 0, 2),
    (1, 1, 0, -1, 5),
    (2, 1, -1, 0, 2),
    (3, 1, 0, -1, 5),
    (1, 3, 1, 0, 2),
    (2, 3, 1, 0, 2),
)
MESH = pl.DeviceIdType.MESH
F32 = jnp.float32
BF16 = jnp.bfloat16


def iota(shape, axis):
    return lax.broadcasted_iota(jnp.int32, shape, axis)


def dot_nt(a, b):
    return lax.dot_general(a, b, (((1,), (1,)), ((), ())), preferred_element_type=F32)


def dot_nn(a, b):
    return lax.dot_general(a, b, (((1,), (0,)), ((), ())), preferred_element_type=F32)


def onehot(mask):
    return jnp.where(mask, F32(1.0), F32(0.0)).astype(BF16)


def kernel(
    emb_ref, lab_ref, req_ref, pl_ref, pr_ref, out_ref,
    line, vis, wout, win, pout, pin, lcol, elab, racc, cacc, rout, rin, cout, cin,
    z_send, z_recv, p_send, p_recv, v_send, v_recv, w_send, w_recv, q_send, q_recv,
    r_send, r_recv, c_send, c_recv,
):
    rows = emb_ref.shape[0]
    half = rows // 2
    me = lax.axis_index("dev")
    core = lax.rem(me, 2)
    z = lax.rem(me // 2, 4)
    ln = me // 8

    def dev(dl, dz, dk):
        to_l = lax.rem(ln + dl + LINES, LINES)
        to_z = lax.rem(z + dz, 4)
        to_k = lax.rem(core + dk, 2)
        return to_l * 8 + to_z * 2 + to_k

    barrier = pltpu.get_barrier_semaphore()
    peers = [dev(0, s % 4, s // 4) for s in range(1, 8)] + [dev(j, 0, 0) for j in range(1, LINES)]
    for peer in peers:
        pl.semaphore_signal(barrier, inc=1, device_id=(peer,), device_id_type=MESH)

    def remote(src, dst, send, recv, to):
        return pltpu.make_async_remote_copy(
            src_ref=src, dst_ref=dst, send_sem=send, recv_sem=recv, device_id=(to,), device_id_type=MESH
        )

    @pl.loop(0, rows // 64)
    def _(i):
        at = pl.ds(pl.multiple_of(i * 64, 64), 64)
        x = emb_ref[at, :].astype(F32)
        total = jnp.sum(x * x, axis=1, keepdims=True)
        line[0, at, :] = (x * lax.rsqrt(total + 1e-06)).astype(BF16)

    expand = onehot((iota((256, 128), 0) // 2 == iota((256, 128), 1)) & (req_ref[...] == iota((256, 128), 0) % 2))
    left = dot_nn(expand, onehot(iota((128, pl_ref.shape[1]), 0) == pl_ref[...])).astype(BF16)
    right = dot_nn(expand, onehot(iota((128, pr_ref.shape[1]), 0) == pr_ref[...])).astype(BF16)
    want = (dot_nt(left, right) + dot_nt(right, left)).astype(BF16)
    labels = jnp.broadcast_to(lab_ref[...].astype(F32), (16, rows)).astype(BF16)
    for j in range(LINES):
        wout[j, 0:16, :] = want[16 * j : 16 * j + 16, :]
        wout[j, 16:32, :] = labels

    pl.semaphore_wait(barrier, len(peers))

    up_a = remote(line.at[0, 0:half], line.at[3, 0:half], z_send.at[0], z_recv.at[0], dev(0, 1, 0))
    dn_b = remote(line.at[0, half:rows], line.at[1, half:rows], z_send.at[1], z_recv.at[1], dev(0, 3, 0))
    up_b = remote(line.at[0, half:rows], line.at[3, half:rows], z_send.at[2], z_recv.at[2], dev(0, 1, 0))
    dn_a = remote(line.at[0, 0:half], line.at[1, 0:half], z_send.at[3], z_recv.at[3], dev(0, 3, 0))
    far_a = remote(line.at[3, 0:half], line.at[2, 0:half], z_send.at[4], z_recv.at[4], dev(0, 1, 0))
    far_b = remote(line.at[1, half:rows], line.at[2, half:rows], z_send.at[5], z_recv.at[5], dev(0, 3, 0))
    share = [
        remote(line.at[r], line.at[4 + r], p_send.at[r], p_recv.at[r], dev(0, 0, 1)) for r in range(4)
    ]
    x = lax.rem(ln, 4)
    y = ln // 4
    piece = rows // CHUNKS

    def visit(number, part):
        at, held, dx, dy, becomes = SPREAD[number]
        rows_of = pl.ds(part * piece, piece)
        src = line.at[0, rows_of] if held == 0 else vis.at[DELTAS.index(held), rows_of]
        m = DELTAS.index(becomes)
        to = (lax.rem(y + dy + 4, 4) * 4 + lax.rem(at + dx + 4, 4)) * 8 + z * 2 + core
        return remote(src, vis.at[m, rows_of], v_send.at[number, part], v_recv.at[m, part], to)

    def spread(held, part):
        for c in range(4):
            numbers = [n for n, entry in enumerate(SPREAD) if entry[0] == c and entry[1] == held]
            if numbers:

                @pl.when(x == c)
                def _():
                    for n in numbers:
                        visit(n, part).start()

    def arrive(delta, part):
        number = [e[4] for e in SPREAD].index(delta)
        visit(number, part).wait_recv()

    tell = [
        remote(
            wout.at[lax.rem(ln + j, LINES)], win.at[LINES - j], w_send.at[j], w_recv.at[LINES - j], dev(j, 0, 0)
        )
        for j in range(1, LINES)
    ]
    back = [(4 - s % 4) % 4 + 4 * (s // 4) for s in range(8)]
    pool = [
        remote(pout, pin.at[back[s]], q_send.at[s], q_recv.at[back[s]], dev(0, s % 4, s // 4)) for s in range(1, 8)
    ]

    for copy in tell:
        copy.start()
    up_a.start()
    dn_b.start()
    share[0].start()
    up_b.start()
    dn_a.start()
    for part in range(CHUNKS):
        spread(0, part)

    total = wout[ln, 0:16, :].astype(F32)
    for copy in tell:
        copy.wait_recv()
    for j in range(1, LINES):
        total = total + win[j, 0:16, :].astype(F32)
    pout[0:16, :] = total.astype(BF16)
    pout[16:32, :] = labels
    for copy in pool:
        copy.start()

    arrive(4, 0)
    spread(4, 0)
    up_a.wait_recv()
    far_a.start()
    dn_b.wait_recv()
    far_b.start()

    for copy in pool:
        copy.wait_recv()
    for s in range(1, 8):
        total = total + pin[s, 0:16, :].astype(F32)
    total = total.astype(BF16)

    eye = iota((BLOCK, BLOCK), 0) == iota((BLOCK, BLOCK), 1)
    ones = jnp.full((BLOCK, BLOCK), 1.0, BF16)
    for s in range(8):
        row = labels[0:1, :] if s == 0 else pin[s, 16:32, :][0:1, :]
        for h in range(2):
            diag = jnp.where(eye, jnp.broadcast_to(row[:, h * BLOCK : (h + 1) * BLOCK].astype(F32), (BLOCK, BLOCK)), F32(0.0))
            lcol[2 * s + h] = dot_nn(diag.astype(BF16), ones)

    for m in range(NV + 1):
        d = 0 if m == 0 else DELTAS[m - 1]
        owner = dev(d, 0, 0)
        pick = onehot(iota((256, rows), 0) == owner * 2 + iota((256, rows), 1) // BLOCK)
        listed = dot_nn(total, pick)
        mine = (labels if m == 0 else win[d % LINES, 16:32, :]).astype(F32)
        elab[m] = jnp.where(listed > 0.5, mine, F32(-1.0))

    for part in range(1, CHUNKS):
        arrive(4, part)
        spread(4, part)
    up_b.wait_recv()
    share[3].start()
    dn_a.wait_recv()
    share[1].start()
    for delta in (1, 3):
        for part in range(CHUNKS):
            arrive(delta, part)
            spread(delta, part)
    far_a.wait_recv()
    far_b.wait_recv()
    share[2].start()

    racc[...] = jnp.full(racc.shape, -1.0, F32)

    def tile(m, s, rhs):
        sims = dot_nt(line[s], rhs[...])
        base = (lax.rem(z + s % 4, 4) * 2 + lax.rem(core + s // 4, 2)) * 2
        cols = []
        for h in range(2):
            lc = lcol[2 * s + h]
            tags = elab[m, pl.ds(base + h, 1), :]
            best = None
            parts = []
            for q in range(2):
                at = slice(q * BLOCK, (q + 1) * BLOCK)
                same = lc == tags[:, at]
                if m == 0 and h == q:
                    same = same & jnp.logical_not(eye & (s == 0))
                val = jnp.where(same, sims[h * BLOCK : (h + 1) * BLOCK, at], F32(-1.0))
                best = val if best is None else jnp.maximum(best, val)
                parts.append(jnp.max(val.reshape(16, 8, BLOCK), axis=0))
            if m > 0:
                racc[2 * s + h] = jnp.maximum(racc[2 * s + h], best)
            cols.append(jnp.concatenate(parts, axis=1))
        cacc[m] = jnp.maximum(cacc[m], jnp.maximum(cols[0], cols[1]))

    def column(m, rhs):
        cacc[m] = jnp.full(cacc.shape[1:], -1.0, F32)

        @pl.loop(0, 8, unroll=8)
        def _(s):
            tile(m, s, rhs)

        top = jnp.max(cacc[m], axis=0, keepdims=True)
        cout[m, 0:1, :] = top[:, 0:BLOCK]
        cout[m, 1:2, :] = top[:, BLOCK:]

    for copy in share:
        copy.wait_recv()
    column(0, line.at[0])
    give = []
    for m, d in enumerate(DELTAS):
        if d in (5, 2):
            for part in range(CHUNKS):
                arrive(d, part)
        column(m + 1, vis.at[m])
        copy = remote(cout.at[m + 1], cin.at[m], c_send.at[m], c_recv.at[m], dev(d, 0, 0))
        copy.start()
        give.append(copy)

    order = [1, 2, 3, 4, 5, 6, 7, 0]
    for s in order:
        for h in range(2):
            flat = jnp.max(jnp.transpose(racc[2 * s + h]), axis=0, keepdims=True)
            rout[s, h : h + 1, :] = flat
        if s > 0:
            copy = remote(rout.at[s], rin.at[back[s]], r_send.at[s], r_recv.at[back[s]], dev(0, s % 4, s // 4))
            copy.start()
            give.append(copy)

    result = jnp.maximum(rout[0], cout[0])
    for copy in give:
        copy.wait_recv()
    for m in range(NV):
        result = jnp.maximum(result, cin[m])
    for s in range(1, 8):
        result = jnp.maximum(result, rin[s])
    out_ref[...] = result
    for copy in [up_a, up_b, dn_a, dn_b, far_a, far_b] + share + tell + pool + give:
        copy.wait_send()
    for c in range(4):

        @pl.when(x == c)
        def _():
            for n, entry in enumerate(SPREAD):
                if entry[0] == c:
                    for part in range(CHUNKS):
                        visit(n, part).wait_send()


def local(embeddings, cluster_id, requests, pair_left, pair_right):
    rows, width = embeddings.shape
    dma = pltpu.SemaphoreType.DMA
    vmem = pltpu.VMEM
    scratch = [
        vmem((8, rows, width), BF16),
        vmem((NV, rows, width), BF16),
        vmem((LINES, 32, 256), BF16),
        vmem((LINES, 32, 256), BF16),
        vmem((32, 256), BF16),
        vmem((8, 32, 256), BF16),
        vmem((16, BLOCK, BLOCK), F32),
        vmem((NV + 1, 16, rows), F32),
        vmem((16, BLOCK, BLOCK), F32),
        vmem((NV + 1, 8, rows), F32),
        vmem((8, 2, BLOCK), F32),
        vmem((8, 2, BLOCK), F32),
        vmem((NV + 1, 2, BLOCK), F32),
        vmem((NV, 2, BLOCK), F32),
    ]
    for sent, received in (
        ((6,), (6,)),
        ((4,), (4,)),
        ((len(SPREAD), CHUNKS), (NV, CHUNKS)),
        ((LINES,), (LINES,)),
        ((8,), (8,)),
        ((8,), (8,)),
        ((NV,), (NV,)),
    ):
        scratch += [dma(sent), dma(received)]
    best = pl.pallas_call(
        kernel,
        out_shape=jax.ShapeDtypeStruct((2, BLOCK), F32),
        in_specs=[pl.BlockSpec(memory_space=pltpu.VMEM)] * 5,
        out_specs=pl.BlockSpec(memory_space=pltpu.VMEM),
        scratch_shapes=scratch,
        compiler_params=pltpu.CompilerParams(
            collective_id=0, has_side_effects=True, vmem_limit_bytes=48 * 1024 * 1024
        ),
        name="band",
    )(
        embeddings,
        cluster_id.reshape(1, -1),
        requests.reshape(1, -1),
        pair_left.reshape(1, -1),
        pair_right.reshape(1, -1),
    )
    return best.reshape(-1)


def solution(mesh):
    in_specs = (P("dev", None), P("dev"), P("dev"), P("dev"), P("dev"))
    out_specs = P("dev")
    return jax.shard_map(local, mesh=mesh, in_specs=in_specs, out_specs=out_specs, check_vma=False)
```

```python
import functools

import jax
import jax.numpy as jnp
from jax import lax
from jax.experimental import pallas as pl
from jax.experimental.pallas import tpu as pltpu
from jax.sharding import PartitionSpec as P

BLOCK = 128
LINES = 16
PARTS = 4
VISITORS = ((4, -1, 5, 3, -5), (4, -3, -1, 5, 3), (-4, -2, 5, -1, 2), (-1, -4, 3, -2, 2))
PASSED = ((1,), (-7, 1), (1, 4), (-3, 4))
NV = len(VISITORS[0])
NP = max(len(p) for p in PASSED)
ROUTE = (
    (0, 0, 0, 0, 1, 0, -1),
    (0, 0, 0, 1, -1, 0, -3),
    (0, 0, 0, 2, 0, -1, 4),
    (0, 1, 0, 0, 1, 0, -1),
    (0, 1, 0, 1, 0, -1, 4),
    (0, 1, 0, 3, -1, 0, 1),
    (0, 2, 0, 0, 0, -1, 4),
    (0, 2, 0, 0, 1, 0, -1),
    (0, 2, 0, 1, -1, 0, 1),
    (0, 2, 0, 3, 0, 1, -4),
    (0, 3, 0, 0, -1, 0, 1),
    (0, 3, 0, 0, 1, 0, 3),
    (0, 3, 0, 1, 0, -1, 4),
    (0, 3, 0, 1, 0, 1, -4),
    (1, 0, 0, 2, -1, 0, -3),
    (1, 0, 0, 3, 0, -1, 4),
    (1, 0, 0, 3, 1, 0, -1),
    (1, 1, 0, 0, 0, -1, 4),
    (1, 1, 0, 2, 1, 0, -1),
    (1, 2, 0, 0, 0, 1, -4),
    (1, 2, 0, 1, 1, 0, -1),
    (1, 2, 0, 2, -1, 0, 1),
    (1, 3, 0, 1, 1, 0, 3),
    (1, 3, 0, 2, 0, -1, 4),
    (1, 3, 0, 2, 0, 1, -4),
    (1, 3, 0, 3, -1, 0, 1),
    (1, 0, 0, 0, 0, -1, 4),
    (1, 0, 0, 2, 1, 0, -1),
    (1, 1, 0, 2, 0, -1, 4),
    (1, 1, 0, 3, 1, 0, -1),
    (1, 2, 0, 1, 0, 1, -4),
    (1, 2, 0, 2, 1, 0, -1),
    (1, 3, 0, 3, 0, 1, -4),
    (1, 0, 0, 1, 0, -1, 4),
    (1, 1, 0, 3, 0, -1, 4),
    (1, 2, 0, 2, 0, 1, -4),
    (1, 2, 0, 3, 1, 0, -1),
    (1, 3, 0, 0, 0, 1, -4),
    (2, 0, 3, 0, 0, 1, -1),
    (2, 1, 1, 1, 0, 1, -3),
    (2, 1, 4, 1, -1, 0, 5),
    (2, 2, 1, 0, 0, -1, 5),
    (2, 0, 1, 3, -1, 0, -2),
    (2, 2, -4, 3, -1, 0, -3),
    (2, 3, -4, 1, 1, 0, -1),
    (2, 3, -3, 1, -1, 0, -2),
    (2, 3, -1, 0, 0, -1, 3),
    (2, 0, 4, 2, 1, 0, 3),
    (2, 1, -1, 0, 1, 0, -2),
    (2, 3, 4, 1, -1, 0, 5),
    (2, 1, 1, 1, 0, -1, 5),
    (2, 2, -1, 0, 1, 0, -2),
    (2, 2, 4, 0, -1, 0, 5),
    (3, 1, 1, 2, 0, 1, -3),
    (3, 1, 4, 0, -1, 0, 5),
    (3, 2, 1, 3, 0, -1, 5),
    (3, 2, -4, 0, -1, 0, -3),
    (3, 3, -4, 2, 1, 0, -1),
    (3, 3, -1, 1, 0, -1, 3),
    (3, 0, 4, 3, 1, 0, 3),
    (3, 1, -1, 3, 1, 0, -2),
    (3, 3, -3, 2, -1, 0, -2),
    (3, 1, 1, 2, 0, -1, 5),
    (3, 2, -1, 2, 1, 0, -2),
    (3, 3, 4, 2, -1, 0, 5),
    (4, 0, -1, 0, 0, 1, -5),
    (4, 0, 5, 1, -1, 0, 2),
    (5, 0, -1, 1, 0, 1, -5),
    (5, 1, -3, 3, 0, 1, -7),
    (5, 1, 4, 2, -1, 0, 5),
    (5, 2, -2, 1, 0, -1, 2),
    (5, 3, -4, 3, 1, 0, -1),
    (5, 3, -1, 2, 0, -1, 3),
    (5, 0, 4, 0, 1, 0, 3),
    (5, 2, -2, 1, -1, 0, -1),
    (6, 0, 5, 0, -1, 0, 2),
    (7, 0, -1, 2, 0, 1, -5),
    (7, 0, -1, 2, 0, -1, 3),
    (7, 1, 4, 3, -1, 0, 5),
    (7, 2, -2, 0, 0, -1, 2),
    (7, 3, 2, 1, 0, 1, -2),
    (7, 1, 3, 2, 1, 0, 2),
    (7, 3, -1, 3, 0, -1, 3),
    (8, 1, -7, 3, 0, 1, 5),
    (8, 0, 5, 2, -1, 0, 2),
    (8, 2, 2, 1, -1, 0, 3),
    (9, 0, -1, 3, 0, 1, -5),
    (9, 0, -1, 3, 0, -1, 3),
    (9, 1, 3, 3, 1, 0, 2),
    (10, 0, 5, 3, -1, 0, 2),
    (10, 3, -2, 1, -1, 0, -1),
)
MESH = pl.DeviceIdType.MESH
F32 = jnp.float32
BF16 = jnp.bfloat16


def iota(shape, axis):
    return lax.broadcasted_iota(jnp.int32, shape, axis)


def dot_nt(a, b):
    return lax.dot_general(a, b, (((1,), (1,)), ((), ())), preferred_element_type=F32)


def dot_nn(a, b):
    return lax.dot_general(a, b, (((1,), (0,)), ((), ())), preferred_element_type=F32)


def onehot(mask):
    return jnp.where(mask, F32(1.0), F32(0.0)).astype(BF16)


def slot_of(c, offset):
    return (VISITORS[c] + PASSED[c]).index(offset)


def choose(x, values):
    value = jnp.int32(values[0])
    for c in range(1, 4):
        value = jnp.where(x == c, jnp.int32(values[c]), value)
    return value


def kernel(
    emb_in, lab_in, req_in, pl_in, pr_in, out_ref,
    emb_ref, lab_ref, req_ref, pl_ref, pr_ref, in_sem,
    line, vis, wout, win, pout, pin, lcol, elab, racc, cacc, rout, rin, cout, cin,
    z_send, z_recv, p_send, p_recv, v_send, v_recv, w_send, w_recv, q_send, q_recv,
    r_send, r_recv, c_send, c_recv,
):
    rows = emb_ref.shape[0]
    half = rows // 2
    piece = rows // PARTS
    me = lax.axis_index("dev")
    core = lax.rem(me, 2)
    z = lax.rem(me // 2, 4)
    ln = me // 8
    x = lax.rem(ln, 4)
    y = ln // 4

    def dev(dl, dz, dk):
        to_l = lax.rem(ln + dl + LINES, LINES)
        to_z = lax.rem(z + dz, 4)
        to_k = lax.rem(core + dk, 2)
        return to_l * 8 + to_z * 2 + to_k

    pairs = ((emb_in, emb_ref), (lab_in, lab_ref), (req_in, req_ref), (pl_in, pl_ref), (pr_in, pr_ref))
    fetch = [pltpu.make_async_copy(src, dst, in_sem.at[i]) for i, (src, dst) in enumerate(pairs)]
    for copy in fetch:
        copy.start()
    barrier = pltpu.get_barrier_semaphore()
    peers = [dev(0, s % 4, s // 4) for s in range(1, 8)] + [dev(j, 0, 0) for j in range(1, LINES)]
    for peer in peers:
        pl.semaphore_signal(barrier, inc=1, device_id=(peer,), device_id_type=MESH)

    def remote(src, dst, send, recv, to):
        return pltpu.make_async_remote_copy(
            src_ref=src, dst_ref=dst, send_sem=send, recv_sem=recv, device_id=(to,), device_id_type=MESH
        )

    cin[...] = jnp.full(cin.shape, -1.0, F32)
    racc[...] = jnp.full(racc.shape, -1.0, F32)
    cacc[...] = jnp.full(cacc.shape, -1.0, F32)

    fetch[0].wait()

    @pl.loop(0, rows // 64)
    def _(i):
        at = pl.ds(pl.multiple_of(i * 64, 64), 64)
        v = emb_ref[at, :].astype(F32)
        total = jnp.sum(v * v, axis=1, keepdims=True)
        line[0, at, :] = (v * lax.rsqrt(total + 1e-06)).astype(BF16)

    for copy in fetch[1:]:
        copy.wait()
    asked = req_ref[...].reshape(1, -1)
    firsts = pl_ref[...].reshape(1, -1)
    seconds = pr_ref[...].reshape(1, -1)
    expand = onehot((iota((256, 128), 0) // 2 == iota((256, 128), 1)) & (asked == iota((256, 128), 0) % 2))
    left = dot_nn(expand, onehot(iota((128, firsts.shape[1]), 0) == firsts)).astype(BF16)
    right = dot_nn(expand, onehot(iota((128, seconds.shape[1]), 0) == seconds)).astype(BF16)
    want = (dot_nt(left, right) + dot_nt(right, left)).astype(BF16)
    tags = lab_ref[...].reshape(1, -1).astype(F32)
    labels = jnp.concatenate(
        [jnp.broadcast_to(tags[:, h * BLOCK : (h + 1) * BLOCK], (8, BLOCK)) for h in range(2)], axis=0
    ).astype(BF16)
    group = iota((1, BLOCK), 1) // 16
    for j in range(LINES):
        offset = jnp.full((1, BLOCK), -1, jnp.int32)
        for m, d in enumerate((0,) + VISITORS[j % 4]):
            offset = jnp.where(group == m, ((j + d) % LINES) * 16 + iota((1, BLOCK), 1) % 16, offset)
        wout[j, 0:16, :] = dot_nn(want[16 * j : 16 * j + 16, :], onehot(iota((256, BLOCK), 0) == offset)).astype(BF16)
        wout[j, 16:32, :] = labels

    pl.semaphore_wait(barrier, len(peers))

    up_a = remote(line.at[0, 0:half], line.at[3, 0:half], z_send.at[0], z_recv.at[0], dev(0, 1, 0))
    dn_b = remote(line.at[0, half:rows], line.at[1, half:rows], z_send.at[1], z_recv.at[1], dev(0, 3, 0))
    up_b = remote(line.at[0, half:rows], line.at[3, half:rows], z_send.at[2], z_recv.at[2], dev(0, 1, 0))
    dn_a = remote(line.at[0, 0:half], line.at[1, 0:half], z_send.at[3], z_recv.at[3], dev(0, 3, 0))
    far_a = remote(line.at[3, 0:half], line.at[2, 0:half], z_send.at[4], z_recv.at[4], dev(0, 1, 0))
    far_b = remote(line.at[1, half:rows], line.at[2, half:rows], z_send.at[5], z_recv.at[5], dev(0, 3, 0))
    share = [
        remote(line.at[r], line.at[4 + r], p_send.at[r], p_recv.at[r], dev(0, 0, 1)) for r in (0, 1, 3)
    ]
    share.insert(2, None)
    far_share = [
        remote(line.at[2, at], line.at[6, at], p_send.at[i], p_recv.at[i], dev(0, 0, 1))
        for i, at in ((2, pl.ds(0, half)), (4, pl.ds(half, half)))
    ]

    waited = {c: set() for c in range(4)}

    def visit(n):
        _, c, held, part, dx, dy, becomes = ROUTE[n]
        at = pl.ds(part * piece, piece)
        src = line.at[0, at] if held == 0 else vis.at[slot_of(c, held), at]
        slot = slot_of((c + dx) % 4, becomes)
        to = (lax.rem(y + dy + 4, 4) * 4 + (c + dx) % 4) * 8 + z * 2 + core
        return remote(src, vis.at[slot, at], v_send.at[n], v_recv.at[slot, part], to)

    def arrive(c, offset, part):
        if (offset, part) not in waited[c]:
            waited[c].add((offset, part))
            at = pl.ds(part * piece, piece)
            slot = slot_of(c, offset)
            remote(
                line.at[0, at], vis.at[slot, at], v_send.at[0], v_recv.at[slot, part], dev(1, 0, 0)
            ).wait_recv()

    def spread(stage):
        for c in range(4):
            numbers = [n for n, e in enumerate(ROUTE) if e[0] == stage and e[1] == c]
            if numbers:

                @pl.when(x == c)
                def _():
                    for n in numbers:
                        if stage > 1:
                            arrive(c, ROUTE[n][2], ROUTE[n][3])
                        visit(n).start()

    def settle(m):
        for c in range(4):
            parts = [p for p in range(PARTS) if (VISITORS[c][m - 1], p) not in waited[c]]
            if parts:

                @pl.when(x == c)
                def _():
                    for p in parts:
                        arrive(c, VISITORS[c][m - 1], p)

    tell = [
        remote(
            wout.at[lax.rem(ln + j, LINES)], win.at[LINES - j], w_send.at[j], w_recv.at[LINES - j], dev(j, 0, 0)
        )
        for j in range(1, LINES)
    ]
    back = [(4 - s % 4) % 4 + 4 * (s // 4) for s in range(8)]
    pool = [
        remote(pout, pin.at[back[s]], q_send.at[s], q_recv.at[back[s]], dev(0, s % 4, s // 4)) for s in range(1, 8)
    ]

    up_a.start()
    dn_b.start()
    share[0].start()
    spread(0)

    for copy in tell:
        copy.start()
    spread(1)
    spread(2)
    total = wout[ln, 0:16, :].astype(F32)
    for copy in tell:
        copy.wait_recv()
    for j in range(1, LINES):
        total = total + win[j, 0:16, :].astype(F32)
    pout[0:16, :] = total.astype(BF16)
    pout[16:32, :] = labels
    for copy in pool:
        copy.start()
    up_b.start()
    dn_a.start()

    up_a.wait_recv()
    far_a.start()
    dn_b.wait_recv()
    far_b.start()
    spread(3)
    spread(4)
    spread(5)
    spread(6)

    for copy in pool:
        copy.wait_recv()
    for s in range(1, 8):
        total = total + pin[s, 0:16, :].astype(F32)
    total = total.astype(BF16)

    eye = iota((BLOCK, BLOCK), 0) == iota((BLOCK, BLOCK), 1)
    ones = jnp.full((BLOCK, BLOCK), 1.0, BF16)
    for s in range(8):
        both = (labels if s == 0 else pin[s, 16:32, :]).astype(F32)
        for h in range(2):
            diag = jnp.where(eye, jnp.broadcast_to(both[8 * h : 8 * h + 1, :], (BLOCK, BLOCK)), F32(0.0))
            lcol[2 * s + h] = dot_nn(diag.astype(BF16), ones)

    offsets = [jnp.int32(0)] + [choose(x, [VISITORS[c][m] for c in range(4)]) for m in range(NV)]
    for m in range(NV + 1):
        column = m * 16 + (z * 2 + core) * 2
        pick = onehot(iota((BLOCK, rows), 0) == column + iota((BLOCK, rows), 1) // BLOCK)
        listed = dot_nn(total, pick)
        theirs = (labels if m == 0 else win[lax.rem(offsets[m] + LINES, LINES), 16:32, :]).astype(F32)
        theirs = jnp.concatenate([theirs[0:1, :], theirs[8:9, :]], axis=1)
        elab[m] = jnp.where(listed > 0.5, theirs, F32(-1.0))

    def tile(m, s):
        rhs = line.at[0] if m == 0 else vis.at[m - 1]
        sims = dot_nt(line[s], rhs[...])
        base = (lax.rem(z + s % 4, 4) * 2 + lax.rem(core + s // 4, 2)) * 2
        cols = []
        for h in range(2):
            lc = lcol[2 * s + h]
            wanted = elab[m, pl.ds(base + h, 1), :]
            best = None
            parts = []
            for q in range(2):
                at = slice(q * BLOCK, (q + 1) * BLOCK)
                same = lc == wanted[:, at]
                if m == 0 and s == 0 and h == q:
                    same = same & jnp.logical_not(eye)
                val = jnp.where(same, sims[h * BLOCK : (h + 1) * BLOCK, at], F32(-1.0))
                best = val if best is None else jnp.maximum(best, val)
                parts.append(jnp.max(val.reshape(16, 8, BLOCK), axis=0))
            if m > 0:
                racc[2 * s + h] = jnp.maximum(racc[2 * s + h], best)
            cols.append(jnp.concatenate(parts, axis=1))
        cacc[m] = jnp.maximum(cacc[m], jnp.maximum(cols[0], cols[1]))

    def tiles(ms, slots):
        for m in ms:
            for s in slots:
                tile(m, s)

    give = []

    def column_out(m):
        top = jnp.max(cacc[m], axis=0, keepdims=True)
        cout[m, 0:1, :] = top[:, 0:BLOCK]
        cout[m, 1:2, :] = top[:, BLOCK:]
        if m > 0:
            at = lax.rem(offsets[m] + LINES, LINES)
            copy = remote(cout.at[m], cin.at[at], c_send.at[m - 1], c_recv.at[at], dev(offsets[m], 0, 0))
            copy.start()
            give.append(copy)

    lines_back = []

    def row_out(s):
        for h in range(2):
            rout[s, h : h + 1, :] = jnp.max(jnp.transpose(racc[2 * s + h]), axis=0, keepdims=True)
        if s > 0:
            copy = remote(rout.at[s], rin.at[back[s]], r_send.at[s], r_recv.at[back[s]], dev(0, s % 4, s // 4))
            copy.start()
            lines_back.append(copy)

    share[0].wait_recv()
    tiles([0], [0, 4])
    spread(7)
    up_b.wait_recv()
    share[3].start()
    dn_a.wait_recv()
    share[1].start()
    settle(1)
    tiles([1], [0, 4])
    spread(8)
    tiles([0], [1, 3])
    spread(9)
    tiles([1], [1, 3])
    spread(10)
    spread(11)
    spread(12)
    share[3].wait_recv()
    share[1].wait_recv()
    tiles([0, 1], [5, 7])
    settle(2)
    tiles([2], [0, 4, 1])
    far_a.wait_recv()
    far_share[0].start()
    far_b.wait_recv()
    far_share[1].start()
    tiles([2], [3, 5, 7])
    settle(3)
    tiles([3], [0, 4, 1, 3, 5, 7])
    tiles([0, 1, 2, 3], [2])
    settle(4)
    tiles([4], [0, 4, 1, 3, 5, 7, 2])
    for copy in far_share:
        copy.wait_recv()
    tiles([0, 1, 2, 3, 4], [6])
    for m in range(5):
        column_out(m)
    settle(5)
    for s in (6, 2, 5, 7, 1, 3, 4, 0):
        tile(5, s)
        row_out(s)
    column_out(5)

    result = jnp.maximum(rout[0], cout[0])
    for c in range(4):
        sources = [d for k in range(4) for d in VISITORS[k] if (k + d) % 4 == c]

        @pl.when(x == c)
        def _():
            for d in sources:
                at = d % LINES
                remote(cout.at[1], cin.at[at], c_send.at[0], c_recv.at[at], dev(1, 0, 0)).wait_recv()

    for copy in lines_back:
        copy.wait_recv()
    for j in range(1, LINES):
        result = jnp.maximum(result, cin[j])
    for s in range(1, 8):
        result = jnp.maximum(result, rin[s])
    out_ref[...] = result
    for copy in [up_a, up_b, dn_a, dn_b, far_a, far_b] + share[:2] + share[3:] + far_share + tell + pool + give + lines_back:
        copy.wait_send()
    for c in range(4):

        @pl.when(x == c)
        def _():
            for offset, part in [(d, p) for d in PASSED[c] for p in range(PARTS)]:
                if any((e[1] + e[4]) % 4 == c and e[6] == offset and e[3] == part for e in ROUTE):
                    arrive(c, offset, part)
            for n, entry in enumerate(ROUTE):
                if entry[1] == c:
                    visit(n).wait_send()


def local(embeddings, cluster_id, requests, pair_left, pair_right):
    rows, width = embeddings.shape
    dma = pltpu.SemaphoreType.DMA
    vmem = pltpu.VMEM
    scratch = [
        vmem((rows, width), BF16),
        vmem(cluster_id.shape, jnp.int32),
        vmem(requests.shape, jnp.int32),
        vmem(pair_left.shape, jnp.int32),
        vmem(pair_right.shape, jnp.int32),
        dma((5,)),
        vmem((8, rows, width), BF16),
        vmem((NV + NP, rows, width), BF16),
        vmem((LINES, 32, BLOCK), BF16),
        vmem((LINES, 32, BLOCK), BF16),
        vmem((32, BLOCK), BF16),
        vmem((8, 32, BLOCK), BF16),
        vmem((16, BLOCK, BLOCK), F32),
        vmem((NV + 1, 16, rows), F32),
        vmem((16, BLOCK, BLOCK), F32),
        vmem((NV + 1, 8, rows), F32),
        vmem((8, 2, BLOCK), F32),
        vmem((8, 2, BLOCK), F32),
        vmem((NV + 1, 2, BLOCK), F32),
        vmem((LINES, 2, BLOCK), F32),
    ]
    for sent, received in (
        ((6,), (6,)),
        ((5,), (5,)),
        ((len(ROUTE),), (NV + NP, PARTS)),
        ((LINES,), (LINES,)),
        ((8,), (8,)),
        ((8,), (8,)),
        ((NV,), (LINES,)),
    ):
        scratch += [dma(sent), dma(received)]
    best = pl.pallas_call(
        kernel,
        out_shape=jax.ShapeDtypeStruct((2, BLOCK), F32),
        in_specs=[pl.BlockSpec(memory_space=pl.ANY)] * 5,
        out_specs=pl.BlockSpec(memory_space=pltpu.VMEM),
        scratch_shapes=scratch,
        compiler_params=pltpu.CompilerParams(
            collective_id=0, has_side_effects=True, vmem_limit_bytes=67_000_000
        ),
        name="band",
    )(embeddings, cluster_id, requests, pair_left, pair_right)
    return best.reshape(-1)


def solution(mesh):
    in_specs = (P("dev", None), P("dev"), P("dev"), P("dev"), P("dev"))
    out_specs = P("dev")
    return jax.shard_map(local, mesh=mesh, in_specs=in_specs, out_specs=out_specs, check_vma=False)
```

```python
import jax
import jax.numpy as jnp
from jax import lax
from jax.experimental import pallas as pl
from jax.experimental.pallas import tpu as pltpu
from jax.sharding import PartitionSpec as P

BLOCK = 128
LINES = 16
PARTS = 4
VISITORS = ((4, -1, 3, -5, -2), (-1, 4, -3, -5, 3), (-1, 4, -5, -2, 5), (-4, 3, -2, -1, 2))
PASSED = ((-4, 1, 5), (1,), (-4, 1), (-8, -3, 4))
NV = len(VISITORS[0])
NP = max(len(p) for p in PASSED)
ROUTE = (
    (0, 0, 0, 0, -1, 0, -3),
    (0, 0, 0, 0, 0, 1, -4),
    (0, 0, 0, 0, 1, 0, -1),
    (0, 0, 0, 2, 0, -1, 4),
    (0, 1, 0, 0, 1, 0, -1),
    (0, 1, 0, 1, -1, 0, 1),
    (0, 1, 0, 3, 0, -1, 4),
    (0, 2, 0, 0, -1, 0, 1),
    (0, 2, 0, 0, 0, -1, 4),
    (0, 2, 0, 1, 0, 1, -4),
    (0, 2, 0, 1, 1, 0, -1),
    (0, 3, 0, 0, 0, -1, 4),
    (0, 3, 0, 0, 1, 0, 3),
    (0, 3, 0, 1, -1, 0, 1),
    (0, 3, 0, 1, 0, 1, -4),
    (1, 0, 0, 0, 0, -1, 4),
    (1, 0, 0, 1, 1, 0, -1),
    (1, 0, 0, 3, -1, 0, -3),
    (1, 0, 0, 3, 0, 1, -4),
    (1, 1, 0, 0, 0, -1, 4),
    (1, 1, 0, 1, 1, 0, -1),
    (1, 1, 0, 2, -1, 0, 1),
    (1, 2, 0, 2, 0, -1, 4),
    (1, 2, 0, 2, 0, 1, -4),
    (1, 2, 0, 3, -1, 0, 1),
    (1, 2, 0, 3, 1, 0, -1),
    (1, 3, 0, 2, -1, 0, 1),
    (1, 3, 0, 2, 0, 1, -4),
    (1, 3, 0, 3, 0, -1, 4),
    (1, 3, 0, 3, 1, 0, 3),
    (1, 0, 0, 1, 0, -1, 4),
    (1, 0, 0, 2, 1, 0, -1),
    (1, 1, 0, 1, 0, -1, 4),
    (1, 1, 0, 2, 1, 0, -1),
    (1, 2, 0, 1, 0, -1, 4),
    (1, 3, 0, 1, 1, 0, 3),
    (1, 3, 0, 3, 0, 1, -4),
    (1, 0, 0, 3, 0, -1, 4),
    (1, 0, 0, 3, 1, 0, -1),
    (1, 1, 0, 2, 0, -1, 4),
    (1, 1, 0, 3, 1, 0, -1),
    (1, 2, 0, 3, 0, -1, 4),
    (2, 1, 1, 0, 0, 1, -3),
    (2, 0, 1, 1, -1, 0, -2),
    (2, 0, 3, 0, 0, 1, -1),
    (2, 1, 4, 3, -1, 0, 5),
    (2, 2, -4, 1, -1, 0, -3),
    (2, 2, -1, 0, 0, 1, -5),
    (2, 2, -1, 0, 1, 0, -2),
    (2, 3, -3, 0, -1, 0, -2),
    (2, 3, -1, 1, 0, -1, 3),
    (2, 2, 4, 0, 1, 0, 3),
    (2, 3, -4, 1, 1, 0, -1),
    (2, 3, 4, 0, -1, 0, 5),
    (2, 0, -4, 0, 1, 0, -5),
    (2, 1, -1, 0, 0, -1, 3),
    (2, 2, 1, 1, 0, -1, 5),
    (2, 0, 4, 2, 1, 0, 3),
    (3, 1, 1, 3, 0, 1, -3),
    (3, 1, -1, 1, 0, 1, -5),
    (3, 0, 1, 2, -1, 0, -2),
    (3, 0, 3, 3, 0, 1, -1),
    (3, 2, -4, 2, -1, 0, -3),
    (3, 2, -1, 1, 0, 1, -5),
    (3, 3, -4, 2, 0, 1, -8),
    (3, 3, -1, 3, 0, -1, 3),
    (3, 1, -1, 1, 1, 0, -2),
    (3, 2, 4, 2, 1, 0, 3),
    (3, 3, -4, 2, 1, 0, -1),
    (3, 3, -3, 3, -1, 0, -2),
    (3, 1, -1, 1, 0, -1, 3),
    (3, 2, 1, 2, 0, -1, 5),
    (3, 3, 4, 3, -1, 0, 5),
    (3, 0, -4, 3, 1, 0, -5),
    (4, 1, -3, 0, -1, 0, -2),
    (5, 1, -1, 2, 0, 1, -5),
    (5, 0, -1, 0, -1, 0, -4),
    (5, 0, -1, 0, 0, 1, -5),
    (5, 1, -3, 1, -1, 0, -2),
    (5, 2, -1, 2, 0, 1, -5),
    (5, 3, -2, 0, 0, -1, 2),
    (5, 0, 5, 3, -1, 0, 2),
    (5, 1, -1, 2, 1, 0, -2),
    (5, 3, -2, 1, 0, -1, 2),
    (6, 1, -3, 3, -1, 0, -2),
    (7, 3, 3, 0, 0, 1, -1),
    (7, 0, -1, 1, 0, 1, -5),
    (7, 1, -3, 2, -1, 0, -2),
    (7, 2, -1, 3, 0, 1, -5),
    (7, 2, -1, 3, 1, 0, -2),
    (7, 3, -8, 2, 1, 0, -5),
    (7, 0, -1, 3, 0, 1, -5),
    (7, 1, -1, 3, 0, -1, 3),
    (7, 3, -2, 2, 0, -1, 2),
    (9, 0, -1, 2, 0, -1, 3),
    (9, 3, 3, 2, 0, 1, -1),
)
MESH = pl.DeviceIdType.MESH
F32 = jnp.float32
BF16 = jnp.bfloat16


def iota(shape, axis):
    return lax.broadcasted_iota(jnp.int32, shape, axis)


def dot_nt(a, b):
    return lax.dot_general(a, b, (((1,), (1,)), ((), ())), preferred_element_type=F32)


def dot_nn(a, b):
    return lax.dot_general(a, b, (((1,), (0,)), ((), ())), preferred_element_type=F32)


def onehot(mask):
    return jnp.where(mask, F32(1.0), F32(0.0)).astype(BF16)


def slot_of(c, offset):
    return (VISITORS[c] + PASSED[c]).index(offset)


def choose(x, values):
    value = jnp.int32(values[0])
    for c in range(1, 4):
        value = jnp.where(x == c, jnp.int32(values[c]), value)
    return value


def kernel(
    emb_in, lab_in, req_in, pl_in, pr_in, out_ref,
    emb_ref, lab_ref, req_ref, pl_ref, pr_ref, in_sem,
    line, vis, wout, win, pout, pin, lcol, elab, racc, cacc, rout, rin, cout, cin,
    z_send, z_recv, p_send, p_recv, v_send, v_recv, w_send, w_recv, q_send, q_recv,
    r_send, r_recv, c_send, c_recv,
):
    rows = emb_ref.shape[0]
    half = rows // 2
    piece = rows // PARTS
    me = lax.axis_index("dev")
    core = lax.rem(me, 2)
    z = lax.rem(me // 2, 4)
    ln = me // 8
    x = lax.rem(ln, 4)
    y = ln // 4

    def dev(dl, dz, dk):
        to_l = lax.rem(ln + dl + LINES, LINES)
        to_z = lax.rem(z + dz, 4)
        to_k = lax.rem(core + dk, 2)
        return to_l * 8 + to_z * 2 + to_k

    pairs = ((emb_in, emb_ref), (lab_in, lab_ref), (req_in, req_ref), (pl_in, pl_ref), (pr_in, pr_ref))
    fetch = [pltpu.make_async_copy(src, dst, in_sem.at[i]) for i, (src, dst) in enumerate(pairs)]
    for copy in fetch:
        copy.start()
    barrier = pltpu.get_barrier_semaphore()
    peers = [dev(0, s % 4, s // 4) for s in range(1, 8)] + [dev(j, 0, 0) for j in range(1, LINES)]
    for peer in peers:
        pl.semaphore_signal(barrier, inc=1, device_id=(peer,), device_id_type=MESH)

    def remote(src, dst, send, recv, to):
        return pltpu.make_async_remote_copy(
            src_ref=src, dst_ref=dst, send_sem=send, recv_sem=recv, device_id=(to,), device_id_type=MESH
        )

    cin[...] = jnp.full(cin.shape, -1.0, F32)
    racc[...] = jnp.full(racc.shape, -1.0, F32)
    cacc[...] = jnp.full(cacc.shape, -1.0, F32)

    fetch[0].wait()

    @pl.loop(0, rows // 64)
    def _(i):
        at = pl.ds(pl.multiple_of(i * 64, 64), 64)
        v = emb_ref[at, :].astype(F32)
        total = jnp.sum(v * v, axis=1, keepdims=True)
        line[0, at, :] = (v * lax.rsqrt(total + 1e-06)).astype(BF16)

    for copy in fetch[1:]:
        copy.wait()
    asked = req_ref[...].reshape(1, -1)
    firsts = pl_ref[...].reshape(1, -1)
    seconds = pr_ref[...].reshape(1, -1)
    expand = onehot((iota((256, 128), 0) // 2 == iota((256, 128), 1)) & (asked == iota((256, 128), 0) % 2))
    left = dot_nn(expand, onehot(iota((128, firsts.shape[1]), 0) == firsts)).astype(BF16)
    right = dot_nn(expand, onehot(iota((128, seconds.shape[1]), 0) == seconds)).astype(BF16)
    want = (dot_nt(left, right) + dot_nt(right, left)).astype(BF16)
    tags = lab_ref[...].reshape(1, -1).astype(F32)
    labels = jnp.concatenate(
        [jnp.broadcast_to(tags[:, h * BLOCK : (h + 1) * BLOCK], (8, BLOCK)) for h in range(2)], axis=0
    ).astype(BF16)
    group = iota((1, BLOCK), 1) // 16
    for j in range(LINES):
        offset = jnp.full((1, BLOCK), -1, jnp.int32)
        for m, d in enumerate((0,) + VISITORS[j % 4]):
            offset = jnp.where(group == m, ((j + d) % LINES) * 16 + iota((1, BLOCK), 1) % 16, offset)
        wout[j, 0:16, :] = dot_nn(want[16 * j : 16 * j + 16, :], onehot(iota((256, BLOCK), 0) == offset)).astype(BF16)
        wout[j, 16:32, :] = labels

    pl.semaphore_wait(barrier, len(peers))

    up_a = remote(line.at[0, 0:half], line.at[3, 0:half], z_send.at[0], z_recv.at[0], dev(0, 1, 0))
    dn_b = remote(line.at[0, half:rows], line.at[1, half:rows], z_send.at[1], z_recv.at[1], dev(0, 3, 0))
    up_b = remote(line.at[0, half:rows], line.at[3, half:rows], z_send.at[2], z_recv.at[2], dev(0, 1, 0))
    dn_a = remote(line.at[0, 0:half], line.at[1, 0:half], z_send.at[3], z_recv.at[3], dev(0, 3, 0))
    far_a = remote(line.at[3, 0:half], line.at[2, 0:half], z_send.at[4], z_recv.at[4], dev(0, 1, 0))
    far_b = remote(line.at[1, half:rows], line.at[2, half:rows], z_send.at[5], z_recv.at[5], dev(0, 3, 0))
    share = [
        remote(line.at[r], line.at[4 + r], p_send.at[r], p_recv.at[r], dev(0, 0, 1)) for r in (0, 1, 3)
    ]
    share.insert(2, None)
    far_share = [
        remote(line.at[2, at], line.at[6, at], p_send.at[i], p_recv.at[i], dev(0, 0, 1))
        for i, at in ((2, pl.ds(0, half)), (4, pl.ds(half, half)))
    ]

    waited = {c: set() for c in range(4)}

    def visit(n):
        _, c, held, part, dx, dy, becomes = ROUTE[n]
        at = pl.ds(part * piece, piece)
        src = line.at[0, at] if held == 0 else vis.at[slot_of(c, held), at]
        slot = slot_of((c + dx) % 4, becomes)
        to = (lax.rem(y + dy + 4, 4) * 4 + (c + dx) % 4) * 8 + z * 2 + core
        return remote(src, vis.at[slot, at], v_send.at[n], v_recv.at[slot, part], to)

    def arrive(c, offset, part):
        if (offset, part) not in waited[c]:
            waited[c].add((offset, part))
            at = pl.ds(part * piece, piece)
            slot = slot_of(c, offset)
            remote(
                line.at[0, at], vis.at[slot, at], v_send.at[0], v_recv.at[slot, part], dev(1, 0, 0)
            ).wait_recv()

    def spread(stage):
        for c in range(4):
            numbers = [n for n, e in enumerate(ROUTE) if e[0] == stage and e[1] == c]
            if numbers:

                @pl.when(x == c)
                def _():
                    for n in numbers:
                        if stage > 1:
                            arrive(c, ROUTE[n][2], ROUTE[n][3])
                        visit(n).start()

    def settle(m):
        for c in range(4):
            parts = [p for p in range(PARTS) if (VISITORS[c][m - 1], p) not in waited[c]]
            if parts:

                @pl.when(x == c)
                def _():
                    for p in parts:
                        arrive(c, VISITORS[c][m - 1], p)

    tell = [
        remote(
            wout.at[lax.rem(ln + j, LINES)], win.at[LINES - j], w_send.at[j], w_recv.at[LINES - j], dev(j, 0, 0)
        )
        for j in range(1, LINES)
    ]
    back = [(4 - s % 4) % 4 + 4 * (s // 4) for s in range(8)]
    pool = [
        remote(pout, pin.at[back[s]], q_send.at[s], q_recv.at[back[s]], dev(0, s % 4, s // 4)) for s in range(1, 8)
    ]

    up_a.start()
    dn_b.start()
    share[0].start()
    spread(0)

    for copy in tell:
        copy.start()
    spread(1)
    spread(2)
    total = wout[ln, 0:16, :].astype(F32)
    for copy in tell:
        copy.wait_recv()
    for j in range(1, LINES):
        total = total + win[j, 0:16, :].astype(F32)
    pout[0:16, :] = total.astype(BF16)
    pout[16:32, :] = labels
    for copy in pool:
        copy.start()
    up_b.start()
    dn_a.start()

    up_a.wait_recv()
    far_a.start()
    dn_b.wait_recv()
    far_b.start()
    spread(3)
    spread(4)
    spread(5)
    spread(6)

    for copy in pool:
        copy.wait_recv()
    for s in range(1, 8):
        total = total + pin[s, 0:16, :].astype(F32)
    total = total.astype(BF16)

    eye = iota((BLOCK, BLOCK), 0) == iota((BLOCK, BLOCK), 1)
    ones = jnp.full((BLOCK, BLOCK), 1.0, BF16)
    for s in range(8):
        both = (labels if s == 0 else pin[s, 16:32, :]).astype(F32)
        for h in range(2):
            diag = jnp.where(eye, jnp.broadcast_to(both[8 * h : 8 * h + 1, :], (BLOCK, BLOCK)), F32(0.0))
            lcol[2 * s + h] = dot_nn(diag.astype(BF16), ones)

    offsets = [jnp.int32(0)] + [choose(x, [VISITORS[c][m] for c in range(4)]) for m in range(NV)]
    for m in range(NV + 1):
        column = m * 16 + (z * 2 + core) * 2
        pick = onehot(iota((BLOCK, rows), 0) == column + iota((BLOCK, rows), 1) // BLOCK)
        listed = dot_nn(total, pick)
        theirs = (labels if m == 0 else win[lax.rem(offsets[m] + LINES, LINES), 16:32, :]).astype(F32)
        theirs = jnp.concatenate([theirs[0:1, :], theirs[8:9, :]], axis=1)
        elab[m] = jnp.where(listed > 0.5, theirs, F32(-1.0))

    def tile(m, s):
        rhs = line.at[0] if m == 0 else vis.at[m - 1]
        sims = dot_nt(line[s], rhs[...])
        base = (lax.rem(z + s % 4, 4) * 2 + lax.rem(core + s // 4, 2)) * 2
        cols = []
        for h in range(2):
            lc = lcol[2 * s + h]
            wanted = elab[m, pl.ds(base + h, 1), :]
            best = None
            parts = []
            for q in range(2):
                at = slice(q * BLOCK, (q + 1) * BLOCK)
                same = lc == wanted[:, at]
                if m == 0 and s == 0 and h == q:
                    same = same & jnp.logical_not(eye)
                val = jnp.where(same, sims[h * BLOCK : (h + 1) * BLOCK, at], F32(-1.0))
                best = val if best is None else jnp.maximum(best, val)
                parts.append(jnp.max(val.reshape(16, 8, BLOCK), axis=0))
            if m > 0 or s in (1, 5):
                racc[2 * s + h] = jnp.maximum(racc[2 * s + h], best)
            cols.append(jnp.concatenate(parts, axis=1))
        cacc[m] = jnp.maximum(cacc[m], jnp.maximum(cols[0], cols[1]))

    def tiles(ms, slots):
        for m in ms:
            for s in slots:
                tile(m, s)

    give = []

    def column_out(m):
        top = jnp.max(cacc[m], axis=0, keepdims=True)
        cout[m, 0:1, :] = top[:, 0:BLOCK]
        cout[m, 1:2, :] = top[:, BLOCK:]
        if m > 0:
            at = lax.rem(offsets[m] + LINES, LINES)
            copy = remote(cout.at[m], cin.at[at], c_send.at[m - 1], c_recv.at[at], dev(offsets[m], 0, 0))
            copy.start()
            give.append(copy)

    lines_back = []

    def row_out(s):
        for h in range(2):
            rout[s, h : h + 1, :] = jnp.max(jnp.transpose(racc[2 * s + h]), axis=0, keepdims=True)
        if s > 0:
            copy = remote(rout.at[s], rin.at[back[s]], r_send.at[s], r_recv.at[back[s]], dev(0, s % 4, s // 4))
            copy.start()
            lines_back.append(copy)

    share[0].wait_recv()
    tiles([0], [0, 4])
    spread(7)
    up_b.wait_recv()
    share[3].start()
    dn_a.wait_recv()
    share[1].start()
    settle(1)
    tiles([1], [0, 4])
    spread(8)
    tiles([0], [1])
    spread(9)
    tiles([1], [1, 3])
    spread(10)
    spread(11)
    spread(12)
    share[3].wait_recv()
    share[1].wait_recv()
    tiles([0], [5])
    tiles([1], [5, 7])
    settle(2)
    tiles([2], [0, 4, 1])
    far_a.wait_recv()
    far_share[0].start()
    far_b.wait_recv()
    far_share[1].start()
    tiles([2], [3, 5, 7])
    settle(3)
    tiles([3], [0, 4, 1, 3, 5, 7])
    tiles([0, 1, 2, 3], [2])
    for copy in far_share:
        copy.wait_recv()
    tiles([0, 1, 2, 3], [6])
    for m in range(4):
        column_out(m)
    settle(4)
    tiles([4], [6, 2, 0, 4, 1, 3, 5, 7])
    column_out(4)
    settle(5)
    for s in (6, 2):
        tile(5, s)
        row_out(s)
    tiles([5], [5, 7, 1, 3, 4, 0])
    column_out(5)
    for s in (5, 7, 1, 3, 4, 0):
        row_out(s)

    result = jnp.maximum(rout[0], cout[0])
    for c in range(4):
        sources = [d for k in range(4) for d in VISITORS[k] if (k + d) % 4 == c]

        @pl.when(x == c)
        def _():
            for d in sources:
                at = d % LINES
                remote(cout.at[1], cin.at[at], c_send.at[0], c_recv.at[at], dev(1, 0, 0)).wait_recv()

    for copy in lines_back:
        copy.wait_recv()
    for j in range(1, LINES):
        result = jnp.maximum(result, cin[j])
    for s in range(1, 8):
        result = jnp.maximum(result, rin[s])
    out_ref[...] = result
    for copy in [up_a, up_b, dn_a, dn_b, far_a, far_b] + share[:2] + share[3:] + far_share + tell + pool + give + lines_back:
        copy.wait_send()
    for c in range(4):

        @pl.when(x == c)
        def _():
            for offset, part in [(d, p) for d in PASSED[c] for p in range(PARTS)]:
                if any((e[1] + e[4]) % 4 == c and e[6] == offset and e[3] == part for e in ROUTE):
                    arrive(c, offset, part)
            for n, entry in enumerate(ROUTE):
                if entry[1] == c:
                    visit(n).wait_send()


def local(embeddings, cluster_id, requests, pair_left, pair_right):
    rows, width = embeddings.shape
    dma = pltpu.SemaphoreType.DMA
    vmem = pltpu.VMEM
    scratch = [
        vmem((rows, width), BF16),
        vmem(cluster_id.shape, jnp.int32),
        vmem(requests.shape, jnp.int32),
        vmem(pair_left.shape, jnp.int32),
        vmem(pair_right.shape, jnp.int32),
        dma((5,)),
        vmem((8, rows, width), BF16),
        vmem((NV + NP, rows, width), BF16),
        vmem((LINES, 32, BLOCK), BF16),
        vmem((LINES, 32, BLOCK), BF16),
        vmem((32, BLOCK), BF16),
        vmem((8, 32, BLOCK), BF16),
        vmem((16, BLOCK, BLOCK), F32),
        vmem((NV + 1, 16, rows), F32),
        vmem((16, BLOCK, BLOCK), F32),
        vmem((NV + 1, 8, rows), F32),
        vmem((8, 2, BLOCK), F32),
        vmem((8, 2, BLOCK), F32),
        vmem((NV + 1, 2, BLOCK), F32),
        vmem((LINES, 2, BLOCK), F32),
    ]
    for sent, received in (
        ((6,), (6,)),
        ((5,), (5,)),
        ((len(ROUTE),), (NV + NP, PARTS)),
        ((LINES,), (LINES,)),
        ((8,), (8,)),
        ((8,), (8,)),
        ((NV,), (LINES,)),
    ):
        scratch += [dma(sent), dma(received)]
    best = pl.pallas_call(
        kernel,
        out_shape=jax.ShapeDtypeStruct((2, BLOCK), F32),
        in_specs=[pl.BlockSpec(memory_space=pl.ANY)] * 5,
        out_specs=pl.BlockSpec(memory_space=pltpu.VMEM),
        scratch_shapes=scratch,
        compiler_params=pltpu.CompilerParams(
            collective_id=0, has_side_effects=True, vmem_limit_bytes=67_000_000
        ),
        name="band",
    )(embeddings, cluster_id, requests, pair_left, pair_right)
    return best.reshape(-1)


def solution(mesh):
    in_specs = (P("dev", None), P("dev"), P("dev"), P("dev"), P("dev"))
    out_specs = P("dev")
    return jax.shard_map(local, mesh=mesh, in_specs=in_specs, out_specs=out_specs, check_vma=False)
```

```python
import jax
import jax.numpy as jnp
from jax import lax
from jax.experimental import pallas as pl
from jax.experimental.pallas import tpu as pltpu
from jax.sharding import PartitionSpec as P

BLOCK = 128
LINES = 16
PARTS = 4
VISITORS = ((4, -1, 3, -5, -2), (-1, 4, -3, -5, 3), (-1, 4, -5, -2, 5), (-4, 3, -2, -1, 2))
PASSED = ((-4, 1, 5), (1,), (-4, 1), (-8, -3, 4))
NV = len(VISITORS[0])
NP = max(len(p) for p in PASSED)
ROUTE = (
    (0, 0, 0, 0, -1, 0, -3),
    (0, 0, 0, 0, 0, 1, -4),
    (0, 0, 0, 0, 1, 0, -1),
    (0, 0, 0, 2, 0, -1, 4),
    (0, 1, 0, 0, 1, 0, -1),
    (0, 1, 0, 1, -1, 0, 1),
    (0, 1, 0, 3, 0, -1, 4),
    (0, 2, 0, 0, -1, 0, 1),
    (0, 2, 0, 0, 0, -1, 4),
    (0, 2, 0, 1, 0, 1, -4),
    (0, 2, 0, 1, 1, 0, -1),
    (0, 3, 0, 0, 0, -1, 4),
    (0, 3, 0, 0, 1, 0, 3),
    (0, 3, 0, 1, -1, 0, 1),
    (0, 3, 0, 1, 0, 1, -4),
    (1, 0, 0, 0, 0, -1, 4),
    (1, 0, 0, 1, 1, 0, -1),
    (1, 0, 0, 3, -1, 0, -3),
    (1, 0, 0, 3, 0, 1, -4),
    (1, 1, 0, 0, 0, -1, 4),
    (1, 1, 0, 1, 1, 0, -1),
    (1, 1, 0, 2, -1, 0, 1),
    (1, 2, 0, 2, 0, -1, 4),
    (1, 2, 0, 2, 0, 1, -4),
    (1, 2, 0, 3, -1, 0, 1),
    (1, 2, 0, 3, 1, 0, -1),
    (1, 3, 0, 2, -1, 0, 1),
    (1, 3, 0, 2, 0, 1, -4),
    (1, 3, 0, 3, 0, -1, 4),
    (1, 3, 0, 3, 1, 0, 3),
    (1, 0, 0, 1, 0, -1, 4),
    (1, 0, 0, 2, 1, 0, -1),
    (1, 1, 0, 1, 0, -1, 4),
    (1, 1, 0, 2, 1, 0, -1),
    (1, 2, 0, 1, 0, -1, 4),
    (1, 3, 0, 1, 1, 0, 3),
    (1, 3, 0, 3, 0, 1, -4),
    (1, 0, 0, 3, 0, -1, 4),
    (1, 0, 0, 3, 1, 0, -1),
    (1, 1, 0, 2, 0, -1, 4),
    (1, 1, 0, 3, 1, 0, -1),
    (1, 2, 0, 3, 0, -1, 4),
    (2, 1, 1, 0, 0, 1, -3),
    (2, 0, 1, 1, -1, 0, -2),
    (2, 0, 3, 0, 0, 1, -1),
    (2, 1, 4, 3, -1, 0, 5),
    (2, 2, -4, 1, -1, 0, -3),
    (2, 2, -1, 0, 0, 1, -5),
    (2, 2, -1, 0, 1, 0, -2),
    (2, 3, -3, 0, -1, 0, -2),
    (2, 3, -1, 1, 0, -1, 3),
    (2, 2, 4, 0, 1, 0, 3),
    (2, 3, -4, 1, 1, 0, -1),
    (2, 3, 4, 0, -1, 0, 5),
    (2, 0, -4, 0, 1, 0, -5),
    (2, 1, -1, 0, 0, -1, 3),
    (2, 2, 1, 1, 0, -1, 5),
    (2, 0, 4, 2, 1, 0, 3),
    (3, 1, 1, 3, 0, 1, -3),
    (3, 1, -1, 1, 0, 1, -5),
    (3, 0, 1, 2, -1, 0, -2),
    (3, 0, 3, 3, 0, 1, -1),
    (3, 2, -4, 2, -1, 0, -3),
    (3, 2, -1, 1, 0, 1, -5),
    (3, 3, -4, 2, 0, 1, -8),
    (3, 3, -1, 3, 0, -1, 3),
    (3, 1, -1, 1, 1, 0, -2),
    (3, 2, 4, 2, 1, 0, 3),
    (3, 3, -4, 2, 1, 0, -1),
    (3, 3, -3, 3, -1, 0, -2),
    (3, 1, -1, 1, 0, -1, 3),
    (3, 2, 1, 2, 0, -1, 5),
    (3, 3, 4, 3, -1, 0, 5),
    (3, 0, -4, 3, 1, 0, -5),
    (4, 1, -3, 0, -1, 0, -2),
    (5, 1, -1, 2, 0, 1, -5),
    (5, 0, -1, 0, -1, 0, -4),
    (5, 0, -1, 0, 0, 1, -5),
    (5, 1, -3, 1, -1, 0, -2),
    (5, 2, -1, 2, 0, 1, -5),
    (5, 3, -2, 0, 0, -1, 2),
    (5, 0, 5, 3, -1, 0, 2),
    (5, 1, -1, 2, 1, 0, -2),
    (5, 3, -2, 1, 0, -1, 2),
    (6, 1, -3, 3, -1, 0, -2),
    (7, 3, 3, 0, 0, 1, -1),
    (7, 0, -1, 1, 0, 1, -5),
    (7, 1, -3, 2, -1, 0, -2),
    (7, 2, -1, 3, 0, 1, -5),
    (7, 2, -1, 3, 1, 0, -2),
    (7, 3, -8, 2, 1, 0, -5),
    (7, 0, -1, 3, 0, 1, -5),
    (7, 1, -1, 3, 0, -1, 3),
    (7, 3, -2, 2, 0, -1, 2),
    (9, 0, -1, 2, 0, -1, 3),
    (9, 3, 3, 2, 0, 1, -1),
)
MESH = pl.DeviceIdType.MESH
F32 = jnp.float32
BF16 = jnp.bfloat16


def iota(shape, axis):
    return lax.broadcasted_iota(jnp.int32, shape, axis)


def dot_nt(a, b):
    return lax.dot_general(a, b, (((1,), (1,)), ((), ())), preferred_element_type=F32)


def dot_nn(a, b):
    return lax.dot_general(a, b, (((1,), (0,)), ((), ())), preferred_element_type=F32)


def onehot(mask):
    return jnp.where(mask, F32(1.0), F32(0.0)).astype(BF16)


def slot_of(c, offset):
    return (VISITORS[c] + PASSED[c]).index(offset)


def choose(x, values):
    value = jnp.int32(values[0])
    for c in range(1, 4):
        value = jnp.where(x == c, jnp.int32(values[c]), value)
    return value


def kernel(
    emb_in, lab_in, req_in, pl_in, pr_in, out_ref,
    emb_ref, lab_ref, req_ref, pl_ref, pr_ref, in_sem,
    line, vis, wout, win, pout, pin, lcol, elab, racc, cacc, rout, rin, cout, cin,
    z_send, z_recv, p_send, p_recv, v_send, v_recv, w_send, w_recv, q_send, q_recv,
    r_send, r_recv, c_send, c_recv,
):
    rows = emb_ref.shape[0]
    half = rows // 2
    piece = rows // PARTS
    me = lax.axis_index("dev")
    core = lax.rem(me, 2)
    z = lax.rem(me // 2, 4)
    ln = me // 8
    x = lax.rem(ln, 4)
    y = ln // 4

    def dev(dl, dz, dk):
        to_l = lax.rem(ln + dl + LINES, LINES)
        to_z = lax.rem(z + dz, 4)
        to_k = lax.rem(core + dk, 2)
        return to_l * 8 + to_z * 2 + to_k

    pairs = ((emb_in, emb_ref), (lab_in, lab_ref), (req_in, req_ref), (pl_in, pl_ref), (pr_in, pr_ref))
    fetch = [pltpu.make_async_copy(src, dst, in_sem.at[i]) for i, (src, dst) in enumerate(pairs)]
    for copy in fetch:
        copy.start()
    barrier = pltpu.get_barrier_semaphore()
    peers = [dev(0, s % 4, s // 4) for s in range(1, 8)] + [dev(j, 0, 0) for j in range(1, LINES)]
    for peer in peers:
        pl.semaphore_signal(barrier, inc=1, device_id=(peer,), device_id_type=MESH)

    def remote(src, dst, send, recv, to):
        return pltpu.make_async_remote_copy(
            src_ref=src, dst_ref=dst, send_sem=send, recv_sem=recv, device_id=(to,), device_id_type=MESH
        )

    cin[...] = jnp.full(cin.shape, -1.0, F32)
    racc[...] = jnp.full(racc.shape, -1.0, F32)
    cacc[...] = jnp.full(cacc.shape, -1.0, F32)

    fetch[0].wait()

    @pl.loop(0, rows // 64)
    def _(i):
        at = pl.ds(pl.multiple_of(i * 64, 64), 64)
        v = emb_ref[at, :].astype(F32)
        total = jnp.sum(v * v, axis=1, keepdims=True)
        line[0, at, :] = (v * lax.rsqrt(total + 1e-06)).astype(BF16)

    for copy in fetch[1:]:
        copy.wait()
    asked = req_ref[...].reshape(1, -1)
    firsts = pl_ref[...].reshape(1, -1)
    seconds = pr_ref[...].reshape(1, -1)
    expand = onehot((iota((256, 128), 0) // 2 == iota((256, 128), 1)) & (asked == iota((256, 128), 0) % 2))
    left = dot_nn(expand, onehot(iota((128, firsts.shape[1]), 0) == firsts)).astype(BF16)
    right = dot_nn(expand, onehot(iota((128, seconds.shape[1]), 0) == seconds)).astype(BF16)
    want = (dot_nt(left, right) + dot_nt(right, left)).astype(BF16)
    tags = lab_ref[...].reshape(1, -1).astype(F32)
    labels = jnp.concatenate(
        [jnp.broadcast_to(tags[:, h * BLOCK : (h + 1) * BLOCK], (8, BLOCK)) for h in range(2)], axis=0
    ).astype(BF16)
    group = iota((1, BLOCK), 1) // 16
    for j in range(LINES):
        offset = jnp.full((1, BLOCK), -1, jnp.int32)
        for m, d in enumerate((0,) + VISITORS[j % 4]):
            offset = jnp.where(group == m, ((j + d) % LINES) * 16 + iota((1, BLOCK), 1) % 16, offset)
        wout[j, 0:16, :] = dot_nn(want[16 * j : 16 * j + 16, :], onehot(iota((256, BLOCK), 0) == offset)).astype(BF16)
        wout[j, 16:32, :] = labels

    pl.semaphore_wait(barrier, len(peers))

    up_a = remote(line.at[0, 0:half], line.at[3, 0:half], z_send.at[0], z_recv.at[0], dev(0, 1, 0))
    dn_b = remote(line.at[0, half:rows], line.at[1, half:rows], z_send.at[1], z_recv.at[1], dev(0, 3, 0))
    up_b = remote(line.at[0, half:rows], line.at[3, half:rows], z_send.at[2], z_recv.at[2], dev(0, 1, 0))
    dn_a = remote(line.at[0, 0:half], line.at[1, 0:half], z_send.at[3], z_recv.at[3], dev(0, 3, 0))
    far_a = remote(line.at[3, 0:half], line.at[2, 0:half], z_send.at[4], z_recv.at[4], dev(0, 1, 0))
    far_b = remote(line.at[1, half:rows], line.at[2, half:rows], z_send.at[5], z_recv.at[5], dev(0, 3, 0))
    share = [
        remote(line.at[r], line.at[4 + r], p_send.at[r], p_recv.at[r], dev(0, 0, 1)) for r in (0, 1, 3)
    ]
    share.insert(2, None)
    far_share = [
        remote(line.at[2, at], line.at[6, at], p_send.at[i], p_recv.at[i], dev(0, 0, 1))
        for i, at in ((2, pl.ds(0, half)), (4, pl.ds(half, half)))
    ]

    waited = {c: set() for c in range(4)}

    def visit(n):
        _, c, held, part, dx, dy, becomes = ROUTE[n]
        at = pl.ds(part * piece, piece)
        src = line.at[0, at] if held == 0 else vis.at[slot_of(c, held), at]
        slot = slot_of((c + dx) % 4, becomes)
        to = (lax.rem(y + dy + 4, 4) * 4 + (c + dx) % 4) * 8 + z * 2 + core
        return remote(src, vis.at[slot, at], v_send.at[n], v_recv.at[slot, part], to)

    def arrive(c, offset, part):
        if (offset, part) not in waited[c]:
            waited[c].add((offset, part))
            at = pl.ds(part * piece, piece)
            slot = slot_of(c, offset)
            remote(
                line.at[0, at], vis.at[slot, at], v_send.at[0], v_recv.at[slot, part], dev(1, 0, 0)
            ).wait_recv()

    def spread(stage):
        for c in range(4):
            numbers = [n for n, e in enumerate(ROUTE) if e[0] == stage and e[1] == c]
            if numbers:

                @pl.when(x == c)
                def _():
                    for n in numbers:
                        if stage > 1:
                            arrive(c, ROUTE[n][2], ROUTE[n][3])
                        visit(n).start()

    def settle(m):
        for c in range(4):
            parts = [p for p in range(PARTS) if (VISITORS[c][m - 1], p) not in waited[c]]
            if parts:

                @pl.when(x == c)
                def _():
                    for p in parts:
                        arrive(c, VISITORS[c][m - 1], p)

    tell = [
        remote(
            wout.at[lax.rem(ln + j, LINES)], win.at[LINES - j], w_send.at[j], w_recv.at[LINES - j], dev(j, 0, 0)
        )
        for j in range(1, LINES)
    ]
    back = [(4 - s % 4) % 4 + 4 * (s // 4) for s in range(8)]
    pool = [
        remote(pout, pin.at[back[s]], q_send.at[s], q_recv.at[back[s]], dev(0, s % 4, s // 4)) for s in range(1, 8)
    ]

    up_a.start()
    dn_b.start()
    for copy in tell:
        copy.start()
    share[0].start()
    spread(0)

    spread(1)
    spread(2)
    total = wout[ln, 0:16, :].astype(F32)
    for copy in tell:
        copy.wait_recv()
    for j in range(1, LINES):
        total = total + win[j, 0:16, :].astype(F32)
    pout[0:16, :] = total.astype(BF16)
    pout[16:32, :] = labels
    for copy in pool:
        copy.start()
    up_b.start()
    dn_a.start()

    up_a.wait_recv()
    far_a.start()
    dn_b.wait_recv()
    far_b.start()
    spread(3)
    spread(4)
    spread(5)
    spread(6)

    for copy in pool:
        copy.wait_recv()
    for s in range(1, 8):
        total = total + pin[s, 0:16, :].astype(F32)
    total = total.astype(BF16)

    eye = iota((BLOCK, BLOCK), 0) == iota((BLOCK, BLOCK), 1)
    ones = jnp.full((BLOCK, BLOCK), 1.0, BF16)
    for s in range(8):
        both = (labels if s == 0 else pin[s, 16:32, :]).astype(F32)
        for h in range(2):
            diag = jnp.where(eye, jnp.broadcast_to(both[8 * h : 8 * h + 1, :], (BLOCK, BLOCK)), F32(0.0))
            lcol[2 * s + h] = dot_nn(diag.astype(BF16), ones)

    offsets = [jnp.int32(0)] + [choose(x, [VISITORS[c][m] for c in range(4)]) for m in range(NV)]
    for m in range(NV + 1):
        column = m * 16 + (z * 2 + core) * 2
        pick = onehot(iota((BLOCK, rows), 0) == column + iota((BLOCK, rows), 1) // BLOCK)
        listed = dot_nn(total, pick)
        theirs = (labels if m == 0 else win[lax.rem(offsets[m] + LINES, LINES), 16:32, :]).astype(F32)
        theirs = jnp.concatenate([theirs[0:1, :], theirs[8:9, :]], axis=1)
        elab[m] = jnp.where(listed > 0.5, theirs, F32(-1.0))

    def tile(m, s):
        rhs = line.at[0] if m == 0 else vis.at[m - 1]
        sims = dot_nt(line[s], rhs[...])
        base = (lax.rem(z + s % 4, 4) * 2 + lax.rem(core + s // 4, 2)) * 2
        cols = []
        for h in range(2):
            lc = lcol[2 * s + h]
            wanted = elab[m, pl.ds(base + h, 1), :]
            best = None
            parts = []
            for q in range(2):
                at = slice(q * BLOCK, (q + 1) * BLOCK)
                same = lc == wanted[:, at]
                if m == 0 and s == 0 and h == q:
                    same = same & jnp.logical_not(eye)
                val = jnp.where(same, sims[h * BLOCK : (h + 1) * BLOCK, at], F32(-1.0))
                best = val if best is None else jnp.maximum(best, val)
                parts.append(jnp.max(val.reshape(16, 8, BLOCK), axis=0))
            if m > 0 or s in (1, 5):
                racc[2 * s + h] = jnp.maximum(racc[2 * s + h], best)
            cols.append(jnp.concatenate(parts, axis=1))
        cacc[m] = jnp.maximum(cacc[m], jnp.maximum(cols[0], cols[1]))

    def tiles(ms, slots):
        for m in ms:
            for s in slots:
                tile(m, s)

    give = []

    def column_out(m):
        top = jnp.max(cacc[m], axis=0, keepdims=True)
        cout[m, 0:1, :] = top[:, 0:BLOCK]
        cout[m, 1:2, :] = top[:, BLOCK:]
        if m > 0:
            at = lax.rem(offsets[m] + LINES, LINES)
            copy = remote(cout.at[m], cin.at[at], c_send.at[m - 1], c_recv.at[at], dev(offsets[m], 0, 0))
            copy.start()
            give.append(copy)

    lines_back = []

    def row_out(s):
        for h in range(2):
            rout[s, h : h + 1, :] = jnp.max(jnp.transpose(racc[2 * s + h]), axis=0, keepdims=True)
        if s > 0:
            copy = remote(rout.at[s], rin.at[back[s]], r_send.at[s], r_recv.at[back[s]], dev(0, s % 4, s // 4))
            copy.start()
            lines_back.append(copy)

    share[0].wait_recv()
    tiles([0], [0, 4])
    spread(7)
    up_b.wait_recv()
    share[3].start()
    dn_a.wait_recv()
    share[1].start()
    settle(1)
    tiles([1], [0, 4])
    spread(8)
    tiles([0], [1])
    spread(9)
    tiles([1], [1, 3])
    share[3].wait_recv()
    share[1].wait_recv()
    tiles([0], [5])
    tiles([1], [5, 7])
    spread(10)
    spread(11)
    spread(12)
    settle(2)
    tiles([2], [0, 4, 1])
    far_a.wait_recv()
    far_share[0].start()
    far_b.wait_recv()
    far_share[1].start()
    tiles([2], [3, 5, 7])
    settle(3)
    tiles([3], [0, 4, 1, 3, 5, 7])
    tiles([0, 1, 2, 3], [2])
    for copy in far_share:
        copy.wait_recv()
    tiles([0, 1, 2, 3], [6])
    for m in range(4):
        column_out(m)
    settle(4)
    tiles([4], [6, 2, 0, 4, 1, 3, 5, 7])
    column_out(4)
    settle(5)
    for s in (6, 2):
        tile(5, s)
        row_out(s)
    tiles([5], [5, 7, 1, 3, 4, 0])
    column_out(5)
    for s in (5, 7, 1, 3, 4, 0):
        row_out(s)

    result = jnp.maximum(rout[0], cout[0])
    for c in range(4):
        sources = [d for k in range(4) for d in VISITORS[k] if (k + d) % 4 == c]

        @pl.when(x == c)
        def _():
            for d in sources:
                at = d % LINES
                remote(cout.at[1], cin.at[at], c_send.at[0], c_recv.at[at], dev(1, 0, 0)).wait_recv()

    for copy in lines_back:
        copy.wait_recv()
    for j in range(1, LINES):
        result = jnp.maximum(result, cin[j])
    for s in range(1, 8):
        result = jnp.maximum(result, rin[s])
    out_ref[...] = result
    for copy in [up_a, up_b, dn_a, dn_b, far_a, far_b] + share[:2] + share[3:] + far_share + tell + pool + give + lines_back:
        copy.wait_send()
    for c in range(4):

        @pl.when(x == c)
        def _():
            for offset, part in [(d, p) for d in PASSED[c] for p in range(PARTS)]:
                if any((e[1] + e[4]) % 4 == c and e[6] == offset and e[3] == part for e in ROUTE):
                    arrive(c, offset, part)
            for n, entry in enumerate(ROUTE):
                if entry[1] == c:
                    visit(n).wait_send()


def local(embeddings, cluster_id, requests, pair_left, pair_right):
    rows, width = embeddings.shape
    dma = pltpu.SemaphoreType.DMA
    vmem = pltpu.VMEM
    scratch = [
        vmem((rows, width), BF16),
        vmem(cluster_id.shape, jnp.int32),
        vmem(requests.shape, jnp.int32),
        vmem(pair_left.shape, jnp.int32),
        vmem(pair_right.shape, jnp.int32),
        dma((5,)),
        vmem((8, rows, width), BF16),
        vmem((NV + NP, rows, width), BF16),
        vmem((LINES, 32, BLOCK), BF16),
        vmem((LINES, 32, BLOCK), BF16),
        vmem((32, BLOCK), BF16),
        vmem((8, 32, BLOCK), BF16),
        vmem((16, BLOCK, BLOCK), F32),
        vmem((NV + 1, 16, rows), F32),
        vmem((16, BLOCK, BLOCK), F32),
        vmem((NV + 1, 8, rows), F32),
        vmem((8, 2, BLOCK), F32),
        vmem((8, 2, BLOCK), F32),
        vmem((NV + 1, 2, BLOCK), F32),
        vmem((LINES, 2, BLOCK), F32),
    ]
    for sent, received in (
        ((6,), (6,)),
        ((5,), (5,)),
        ((len(ROUTE),), (NV + NP, PARTS)),
        ((LINES,), (LINES,)),
        ((8,), (8,)),
        ((8,), (8,)),
        ((NV,), (LINES,)),
    ):
        scratch += [dma(sent), dma(received)]
    best = pl.pallas_call(
        kernel,
        out_shape=jax.ShapeDtypeStruct((2, BLOCK), F32),
        in_specs=[pl.BlockSpec(memory_space=pl.ANY)] * 5,
        out_specs=pl.BlockSpec(memory_space=pltpu.VMEM),
        scratch_shapes=scratch,
        compiler_params=pltpu.CompilerParams(
            collective_id=0, has_side_effects=True, vmem_limit_bytes=67_000_000
        ),
        name="band",
    )(embeddings, cluster_id, requests, pair_left, pair_right)
    return best.reshape(-1)


def solution(mesh):
    in_specs = (P("dev", None), P("dev"), P("dev"), P("dev"), P("dev"))
    out_specs = P("dev")
    return jax.shard_map(local, mesh=mesh, in_specs=in_specs, out_specs=out_specs, check_vma=False)
```

```python
import jax
import jax.numpy as jnp
from jax import lax
from jax.experimental import pallas as pl
from jax.experimental.pallas import tpu as pltpu
from jax.sharding import PartitionSpec as P

BLOCK = 128
LINES = 16
PARTS = 4
VISITORS = ((4, -1, 5, -5, -2), (4, -3, -1, 3, 2), (-1, 4, 5, -5, -2), (-3, -4, 3, -1, 2))
PASSED = ((1, 3), (1,), (-4, 1), (-8, -5, -2, 4))
NV = len(VISITORS[0])
NP = max(len(p) for p in PASSED)
ROUTE = (
    (0, 0, 0, 0, 1, 0, -1),
    (0, 0, 0, 2, 0, -1, 4),
    (0, 0, 0, 3, -1, 0, -3),
    (0, 1, 0, 0, 0, -1, 4),
    (0, 1, 0, 2, 1, 0, -1),
    (0, 1, 0, 3, -1, 0, 1),
    (0, 2, 0, 0, -1, 0, 1),
    (0, 2, 0, 1, 1, 0, -1),
    (0, 2, 0, 3, 0, -1, 4),
    (0, 2, 0, 3, 0, 1, -4),
    (0, 3, 0, 0, 0, -1, 4),
    (0, 3, 0, 1, -1, 0, 1),
    (0, 3, 0, 1, 0, 1, -4),
    (0, 3, 0, 3, 1, 0, 3),
    (1, 0, 0, 0, -1, 0, -3),
    (1, 0, 0, 1, 1, 0, -1),
    (1, 0, 0, 3, 0, -1, 4),
    (1, 1, 0, 0, 1, 0, -1),
    (1, 1, 0, 1, 0, -1, 4),
    (1, 2, 0, 0, 0, -1, 4),
    (1, 2, 0, 1, -1, 0, 1),
    (1, 2, 0, 2, 0, 1, -4),
    (1, 2, 0, 2, 1, 0, -1),
    (1, 3, 0, 0, 1, 0, 3),
    (1, 3, 0, 2, -1, 0, 1),
    (1, 3, 0, 2, 0, 1, -4),
    (1, 0, 0, 0, 0, -1, 4),
    (1, 0, 0, 1, -1, 0, -3),
    (1, 1, 0, 1, 1, 0, -1),
    (1, 1, 0, 2, 0, -1, 4),
    (1, 2, 0, 0, 1, 0, -1),
    (1, 2, 0, 1, 0, -1, 4),
    (1, 3, 0, 3, -1, 0, 1),
    (1, 3, 0, 3, 0, 1, -4),
    (1, 0, 0, 1, 0, -1, 4),
    (1, 0, 0, 2, -1, 0, -3),
    (1, 1, 0, 3, 0, -1, 4),
    (1, 1, 0, 3, 1, 0, -1),
    (2, 0, 3, 3, 0, 1, -1),
    (2, 1, 1, 0, 0, 1, -3),
    (2, 1, 4, 0, -1, 0, 5),
    (2, 3, 4, 0, 0, -1, -8),
    (2, 0, 4, 2, 1, 0, 3),
    (2, 2, -4, 3, -1, 0, -3),
    (2, 3, -4, 1, 1, 0, -1),
    (2, 2, -1, 2, 1, 0, -2),
    (2, 2, 1, 1, -1, 0, 2),
    (2, 2, 1, 1, 0, -1, 5),
    (2, 3, -1, 1, 0, -1, 3),
    (2, 3, -1, 1, 0, 1, -5),
    (2, 3, 4, 0, -1, 0, 5),
    (2, 0, 1, 3, 0, -1, 5),
    (2, 1, -1, 0, 0, -1, 3),
    (2, 1, -1, 0, 1, 0, -2),
    (2, 2, -1, 2, 0, 1, -5),
    (2, 2, 4, 3, 1, 0, 3),
    (2, 3, -3, 3, -1, 0, -2),
    (2, 0, 3, 3, 1, 0, 2),
    (3, 0, 3, 0, 0, 1, -1),
    (3, 1, 1, 1, 0, 1, -3),
    (3, 1, 4, 1, -1, 0, 5),
    (3, 2, -1, 0, 0, 1, -5),
    (3, 3, -1, 2, 0, -1, 3),
    (3, 0, 4, 3, 1, 0, 3),
    (3, 3, -4, 2, 1, 0, -1),
    (3, 0, 3, 0, 1, 0, 2),
    (3, 2, -4, 2, -1, 0, -3),
    (3, 2, 1, 2, 0, -1, 5),
    (3, 3, -1, 2, 0, 1, -5),
    (3, 1, -1, 1, 0, -1, 3),
    (3, 1, -1, 1, 1, 0, -2),
    (3, 2, 1, 2, -1, 0, 2),
    (3, 2, 4, 0, 1, 0, 3),
    (4, 0, -1, 3, 0, 1, -5),
    (4, 0, 5, 0, -1, 0, 2),
    (4, 1, -3, 0, -1, 0, -2),
    (4, 3, -8, 0, 0, -1, -4),
    (4, 3, -8, 0, 1, 0, -5),
    (5, 0, -1, 1, 0, 1, -5),
    (5, 1, 3, 2, 0, 1, -1),
    (5, 1, 4, 2, -1, 0, 5),
    (5, 2, -1, 1, 0, 1, -5),
    (5, 1, -3, 3, -1, 0, -2),
    (5, 2, 1, 3, 0, -1, 5),
    (6, 0, 5, 1, -1, 0, 2),
    (6, 3, 3, 2, -1, 0, 4),
    (7, 0, -1, 2, 0, 1, -5),
    (7, 1, 3, 3, 0, 1, -1),
    (7, 2, -1, 3, 0, 1, -5),
    (7, 3, -5, 1, 1, 0, -2),
    (7, 3, -2, 2, 0, -1, 2),
    (8, 1, -1, 2, 1, 0, -2),
    (9, 3, 3, 3, 0, 1, -1),
    (9, 0, 5, 3, -1, 0, 2),
    (9, 3, -5, 2, 1, 0, -2),
)
MESH = pl.DeviceIdType.MESH
F32 = jnp.float32
BF16 = jnp.bfloat16


def iota(shape, axis):
    return lax.broadcasted_iota(jnp.int32, shape, axis)


def dot_nt(a, b):
    return lax.dot_general(a, b, (((1,), (1,)), ((), ())), preferred_element_type=F32)


def dot_nn(a, b):
    return lax.dot_general(a, b, (((1,), (0,)), ((), ())), preferred_element_type=F32)


def onehot(mask):
    return jnp.where(mask, F32(1.0), F32(0.0)).astype(BF16)


def slot_of(c, offset):
    return (VISITORS[c] + PASSED[c]).index(offset)


def choose(x, values):
    value = jnp.int32(values[0])
    for c in range(1, 4):
        value = jnp.where(x == c, jnp.int32(values[c]), value)
    return value


def kernel(
    emb_in, lab_in, req_in, pl_in, pr_in, out_ref,
    emb_ref, lab_ref, req_ref, pl_ref, pr_ref, in_sem,
    line, vis, wout, win, pout, pin, lcol, elab, racc, cacc, rout, rin, cout, cin,
    z_send, z_recv, p_send, p_recv, v_send, v_recv, w_send, w_recv, q_send, q_recv,
    r_send, r_recv, c_send, c_recv,
):
    rows = emb_ref.shape[0]
    half = rows // 2
    piece = rows // PARTS
    me = lax.axis_index("dev")
    core = lax.rem(me, 2)
    z = lax.rem(me // 2, 4)
    ln = me // 8
    x = lax.rem(ln, 4)
    y = ln // 4

    def dev(dl, dz, dk):
        to_l = lax.rem(ln + dl + LINES, LINES)
        to_z = lax.rem(z + dz, 4)
        to_k = lax.rem(core + dk, 2)
        return to_l * 8 + to_z * 2 + to_k

    pairs = ((emb_in, emb_ref), (lab_in, lab_ref), (req_in, req_ref), (pl_in, pl_ref), (pr_in, pr_ref))
    fetch = [pltpu.make_async_copy(src, dst, in_sem.at[i]) for i, (src, dst) in enumerate(pairs)]
    for copy in fetch:
        copy.start()
    barrier = pltpu.get_barrier_semaphore()
    peers = [dev(0, s % 4, s // 4) for s in range(1, 8)] + [dev(j, 0, 0) for j in range(1, LINES)]
    for peer in peers:
        pl.semaphore_signal(barrier, inc=1, device_id=(peer,), device_id_type=MESH)

    def remote(src, dst, send, recv, to):
        return pltpu.make_async_remote_copy(
            src_ref=src, dst_ref=dst, send_sem=send, recv_sem=recv, device_id=(to,), device_id_type=MESH
        )

    cin[...] = jnp.full(cin.shape, -1.0, F32)
    racc[...] = jnp.full(racc.shape, -1.0, F32)
    cacc[...] = jnp.full(cacc.shape, -1.0, F32)

    fetch[0].wait()

    @pl.loop(0, rows // 64)
    def _(i):
        at = pl.ds(pl.multiple_of(i * 64, 64), 64)
        v = emb_ref[at, :].astype(F32)
        total = jnp.sum(v * v, axis=1, keepdims=True)
        line[0, at, :] = (v * lax.rsqrt(total + 1e-06)).astype(BF16)

    for copy in fetch[1:]:
        copy.wait()
    asked = req_ref[...].reshape(1, -1)
    firsts = pl_ref[...].reshape(1, -1)
    seconds = pr_ref[...].reshape(1, -1)
    expand = onehot((iota((256, 128), 0) // 2 == iota((256, 128), 1)) & (asked == iota((256, 128), 0) % 2))
    left = dot_nn(expand, onehot(iota((128, firsts.shape[1]), 0) == firsts)).astype(BF16)
    right = dot_nn(expand, onehot(iota((128, seconds.shape[1]), 0) == seconds)).astype(BF16)
    want = (dot_nt(left, right) + dot_nt(right, left)).astype(BF16)
    tags = lab_ref[...].reshape(1, -1).astype(F32)
    labels = jnp.concatenate(
        [jnp.broadcast_to(tags[:, h * BLOCK : (h + 1) * BLOCK], (8, BLOCK)) for h in range(2)], axis=0
    ).astype(BF16)
    group = iota((1, BLOCK), 1) // 16
    for j in range(LINES):
        offset = jnp.full((1, BLOCK), -1, jnp.int32)
        for m, d in enumerate((0,) + VISITORS[j % 4]):
            offset = jnp.where(group == m, ((j + d) % LINES) * 16 + iota((1, BLOCK), 1) % 16, offset)
        wout[j, 0:16, :] = dot_nn(want[16 * j : 16 * j + 16, :], onehot(iota((256, BLOCK), 0) == offset)).astype(BF16)
        wout[j, 16:32, :] = labels

    pl.semaphore_wait(barrier, len(peers))

    up_a = remote(line.at[0, 0:half], line.at[3, 0:half], z_send.at[0], z_recv.at[0], dev(0, 1, 0))
    dn_b = remote(line.at[0, half:rows], line.at[1, half:rows], z_send.at[1], z_recv.at[1], dev(0, 3, 0))
    up_b = remote(line.at[0, half:rows], line.at[3, half:rows], z_send.at[2], z_recv.at[2], dev(0, 1, 0))
    dn_a = remote(line.at[0, 0:half], line.at[1, 0:half], z_send.at[3], z_recv.at[3], dev(0, 3, 0))
    far_a = remote(line.at[3, 0:half], line.at[2, 0:half], z_send.at[4], z_recv.at[4], dev(0, 1, 0))
    far_b = remote(line.at[1, half:rows], line.at[2, half:rows], z_send.at[5], z_recv.at[5], dev(0, 3, 0))
    share = [
        remote(line.at[r], line.at[4 + r], p_send.at[r], p_recv.at[r], dev(0, 0, 1)) for r in (0, 1, 3)
    ]
    share.insert(2, None)
    far_share = [
        remote(line.at[2, at], line.at[6, at], p_send.at[i], p_recv.at[i], dev(0, 0, 1))
        for i, at in ((2, pl.ds(0, half)), (4, pl.ds(half, half)))
    ]

    waited = {c: set() for c in range(4)}

    def visit(n):
        _, c, held, part, dx, dy, becomes = ROUTE[n]
        at = pl.ds(part * piece, piece)
        src = line.at[0, at] if held == 0 else vis.at[slot_of(c, held), at]
        slot = slot_of((c + dx) % 4, becomes)
        to = (lax.rem(y + dy + 4, 4) * 4 + (c + dx) % 4) * 8 + z * 2 + core
        return remote(src, vis.at[slot, at], v_send.at[n], v_recv.at[slot, part], to)

    def arrive(c, offset, part):
        if (offset, part) not in waited[c]:
            waited[c].add((offset, part))
            at = pl.ds(part * piece, piece)
            slot = slot_of(c, offset)
            remote(
                line.at[0, at], vis.at[slot, at], v_send.at[0], v_recv.at[slot, part], dev(1, 0, 0)
            ).wait_recv()

    def spread(stage):
        for c in range(4):
            numbers = [n for n, e in enumerate(ROUTE) if e[0] == stage and e[1] == c]
            if numbers:

                @pl.when(x == c)
                def _():
                    for n in numbers:
                        if stage > 1:
                            arrive(c, ROUTE[n][2], ROUTE[n][3])
                        visit(n).start()

    def settle(m):
        for c in range(4):
            parts = [p for p in range(PARTS) if (VISITORS[c][m - 1], p) not in waited[c]]
            if parts:

                @pl.when(x == c)
                def _():
                    for p in parts:
                        arrive(c, VISITORS[c][m - 1], p)

    tell = [
        remote(
            wout.at[lax.rem(ln + j, LINES)], win.at[LINES - j], w_send.at[j], w_recv.at[LINES - j], dev(j, 0, 0)
        )
        for j in range(1, LINES)
    ]
    back = [(4 - s % 4) % 4 + 4 * (s // 4) for s in range(8)]
    pool = [
        remote(pout, pin.at[back[s]], q_send.at[s], q_recv.at[back[s]], dev(0, s % 4, s // 4)) for s in range(1, 8)
    ]

    up_a.start()
    dn_b.start()
    for copy in tell:
        copy.start()
    share[0].start()
    spread(0)

    spread(1)
    spread(2)
    total = wout[ln, 0:16, :].astype(F32)
    for copy in tell:
        copy.wait_recv()
    for j in range(1, LINES):
        total = total + win[j, 0:16, :].astype(F32)
    pout[0:16, :] = total.astype(BF16)
    pout[16:32, :] = labels
    for copy in pool:
        copy.start()
    up_b.start()
    dn_a.start()

    up_a.wait_recv()
    far_a.start()
    dn_b.wait_recv()
    far_b.start()
    spread(3)
    spread(4)
    spread(5)
    spread(6)

    for copy in pool:
        copy.wait_recv()
    for s in range(1, 8):
        total = total + pin[s, 0:16, :].astype(F32)
    total = total.astype(BF16)

    eye = iota((BLOCK, BLOCK), 0) == iota((BLOCK, BLOCK), 1)
    ones = jnp.full((BLOCK, BLOCK), 1.0, BF16)
    for s in range(8):
        both = (labels if s == 0 else pin[s, 16:32, :]).astype(F32)
        for h in range(2):
            diag = jnp.where(eye, jnp.broadcast_to(both[8 * h : 8 * h + 1, :], (BLOCK, BLOCK)), F32(0.0))
            lcol[2 * s + h] = dot_nn(diag.astype(BF16), ones)

    offsets = [jnp.int32(0)] + [choose(x, [VISITORS[c][m] for c in range(4)]) for m in range(NV)]
    for m in range(NV + 1):
        column = m * 16 + (z * 2 + core) * 2
        pick = onehot(iota((BLOCK, rows), 0) == column + iota((BLOCK, rows), 1) // BLOCK)
        listed = dot_nn(total, pick)
        theirs = (labels if m == 0 else win[lax.rem(offsets[m] + LINES, LINES), 16:32, :]).astype(F32)
        theirs = jnp.concatenate([theirs[0:1, :], theirs[8:9, :]], axis=1)
        elab[m] = jnp.where(listed > 0.5, theirs, F32(-1.0))

    def tile(m, s):
        rhs = line.at[0] if m == 0 else vis.at[m - 1]
        sims = dot_nt(line[s], rhs[...])
        base = (lax.rem(z + s % 4, 4) * 2 + lax.rem(core + s // 4, 2)) * 2
        cols = []
        for h in range(2):
            lc = lcol[2 * s + h]
            wanted = elab[m, pl.ds(base + h, 1), :]
            best = None
            parts = []
            for q in range(2):
                at = slice(q * BLOCK, (q + 1) * BLOCK)
                same = lc == wanted[:, at]
                if m == 0 and s == 0 and h == q:
                    same = same & jnp.logical_not(eye)
                val = jnp.where(same, sims[h * BLOCK : (h + 1) * BLOCK, at], F32(-1.0))
                best = val if best is None else jnp.maximum(best, val)
                parts.append(jnp.max(val.reshape(16, 8, BLOCK), axis=0))
            if m > 0 or s in (1, 5):
                racc[2 * s + h] = jnp.maximum(racc[2 * s + h], best)
            cols.append(jnp.concatenate(parts, axis=1))
        cacc[m] = jnp.maximum(cacc[m], jnp.maximum(cols[0], cols[1]))

    def tiles(ms, slots):
        for m in ms:
            for s in slots:
                tile(m, s)

    give = []

    def column_out(m):
        top = jnp.max(cacc[m], axis=0, keepdims=True)
        cout[m, 0:1, :] = top[:, 0:BLOCK]
        cout[m, 1:2, :] = top[:, BLOCK:]
        if m > 0:
            at = lax.rem(offsets[m] + LINES, LINES)
            copy = remote(cout.at[m], cin.at[at], c_send.at[m - 1], c_recv.at[at], dev(offsets[m], 0, 0))
            copy.start()
            give.append(copy)

    lines_back = []

    def row_out(s):
        for h in range(2):
            rout[s, h : h + 1, :] = jnp.max(jnp.transpose(racc[2 * s + h]), axis=0, keepdims=True)
        if s > 0:
            copy = remote(rout.at[s], rin.at[back[s]], r_send.at[s], r_recv.at[back[s]], dev(0, s % 4, s // 4))
            copy.start()
            lines_back.append(copy)

    share[0].wait_recv()
    tiles([0], [0, 4])
    spread(7)
    up_b.wait_recv()
    share[3].start()
    dn_a.wait_recv()
    share[1].start()
    settle(1)
    tiles([1], [0, 4])
    spread(8)
    tiles([0], [1])
    spread(9)
    tiles([1], [1, 3])
    share[3].wait_recv()
    share[1].wait_recv()
    tiles([0], [5])
    tiles([1], [5, 7])
    spread(10)
    spread(11)
    spread(12)
    settle(2)
    tiles([2], [0, 4])
    far_a.wait_recv()
    far_share[0].start()
    far_b.wait_recv()
    far_share[1].start()
    tiles([2], [1, 3, 5, 7])
    tiles([0, 1, 2], [2])
    settle(3)
    tiles([3], [0, 4, 1, 3, 5, 7])
    tiles([3], [2])
    for copy in far_share:
        copy.wait_recv()
    tiles([0, 1, 2, 3], [6])
    for m in range(4):
        column_out(m)
    settle(4)
    tiles([4], [6, 2, 0, 4, 1, 3, 5, 7])
    column_out(4)
    settle(5)
    for s in (6, 2):
        tile(5, s)
        row_out(s)
    tiles([5], [5, 7, 1, 3, 4, 0])
    column_out(5)
    for s in (5, 7, 1, 3, 4, 0):
        row_out(s)

    result = jnp.maximum(rout[0], cout[0])
    for c in range(4):
        sources = [d for k in range(4) for d in VISITORS[k] if (k + d) % 4 == c]

        @pl.when(x == c)
        def _():
            for d in sources:
                at = d % LINES
                remote(cout.at[1], cin.at[at], c_send.at[0], c_recv.at[at], dev(1, 0, 0)).wait_recv()

    for copy in lines_back:
        copy.wait_recv()
    for j in range(1, LINES):
        result = jnp.maximum(result, cin[j])
    for s in range(1, 8):
        result = jnp.maximum(result, rin[s])
    out_ref[...] = result
    for copy in [up_a, up_b, dn_a, dn_b, far_a, far_b] + share[:2] + share[3:] + far_share + tell + pool + give + lines_back:
        copy.wait_send()
    for c in range(4):

        @pl.when(x == c)
        def _():
            for offset, part in [(d, p) for d in PASSED[c] for p in range(PARTS)]:
                if any((e[1] + e[4]) % 4 == c and e[6] == offset and e[3] == part for e in ROUTE):
                    arrive(c, offset, part)
            for n, entry in enumerate(ROUTE):
                if entry[1] == c:
                    visit(n).wait_send()


def local(embeddings, cluster_id, requests, pair_left, pair_right):
    rows, width = embeddings.shape
    dma = pltpu.SemaphoreType.DMA
    vmem = pltpu.VMEM
    scratch = [
        vmem((rows, width), BF16),
        vmem(cluster_id.shape, jnp.int32),
        vmem(requests.shape, jnp.int32),
        vmem(pair_left.shape, jnp.int32),
        vmem(pair_right.shape, jnp.int32),
        dma((5,)),
        vmem((8, rows, width), BF16),
        vmem((NV + NP, rows, width), BF16),
        vmem((LINES, 32, BLOCK), BF16),
        vmem((LINES, 32, BLOCK), BF16),
        vmem((32, BLOCK), BF16),
        vmem((8, 32, BLOCK), BF16),
        vmem((16, BLOCK, BLOCK), F32),
        vmem((NV + 1, 16, rows), F32),
        vmem((16, BLOCK, BLOCK), F32),
        vmem((NV + 1, 8, rows), F32),
        vmem((8, 2, BLOCK), F32),
        vmem((8, 2, BLOCK), F32),
        vmem((NV + 1, 2, BLOCK), F32),
        vmem((LINES, 2, BLOCK), F32),
    ]
    for sent, received in (
        ((6,), (6,)),
        ((5,), (5,)),
        ((len(ROUTE),), (NV + NP, PARTS)),
        ((LINES,), (LINES,)),
        ((8,), (8,)),
        ((8,), (8,)),
        ((NV,), (LINES,)),
    ):
        scratch += [dma(sent), dma(received)]
    best = pl.pallas_call(
        kernel,
        out_shape=jax.ShapeDtypeStruct((2, BLOCK), F32),
        in_specs=[pl.BlockSpec(memory_space=pl.ANY)] * 5,
        out_specs=pl.BlockSpec(memory_space=pltpu.VMEM),
        scratch_shapes=scratch,
        compiler_params=pltpu.CompilerParams(
            collective_id=0, has_side_effects=True, vmem_limit_bytes=67_000_000
        ),
        name="band",
    )(embeddings, cluster_id, requests, pair_left, pair_right)
    return best.reshape(-1)


def solution(mesh):
    in_specs = (P("dev", None), P("dev"), P("dev"), P("dev"), P("dev"))
    out_specs = P("dev")
    return jax.shard_map(local, mesh=mesh, in_specs=in_specs, out_specs=out_specs, check_vma=False)
```
